128 devices in a mesh: member: 8 (over y, core), fsdp: 16 (over z, x).
Axes of the slice: x: 4, y: 4, z: 4, core: 2. Of those that a mesh axis runs over, the one named last changes fastest.
Arguments:
- tokens: bfloat16 [3072, 4096], P('fsdp'), may hold values from -6 to 6
- routes: int32 [3072, 2], P('fsdp'), may hold values from 0 to 7, all different within a row; in each aligned block of 192 rows (0 to 191, 192 to 383, ...) at most 72 rows name the same one
- combine: float32 [3072, 2], P('fsdp'), may hold values from 0.25 to 1
- gate_weight: bfloat16 [8, 11008, 4096], P('member', None, 'fsdp'), may hold values from -0.09375 to 0.09375
- up_weight: bfloat16 [8, 11008, 4096], P('member', None, 'fsdp'), may hold values from -0.09375 to 0.09375
- down_weight: bfloat16 [8, 11008, 4096], P('member', None, 'fsdp'), may hold values from -0.0546875 to 0.0546875
Outputs:
- mixed: bfloat16 [3072, 4096], P('fsdp', 'member')
The draws below stay inside these ranges and needn't reach their ends.
Inputs may be any that keep to these rules, and one draw needn't show every extreme that they name: `routes`: each row names two different experts. In each aligned block of 192 rows no expert is named by more than 72 rows, a bound that some block reaches.
All inputs are finite; a program needn't handle non-finite values.
Results may differ from the reference program's by a relative error of at most 0.0049.
Values may be sent and summed in bfloat16 or wider, within the bound.
A program may use at most 128 MiB of HBM per device.

```python
import math
import jax
import jax.numpy as jnp
import numpy as np
from jax import lax

D = 4096
FF = 11008
TOK_DEV = 192
EXPERTS = 8
MOST = 72
TOKENS = 3072
N_FSDP = 16


def level_of(key, dims, split, smallest, high):
    factor_of, own = 1.0, jax.random.fold_in(key, 6)
    for position, parts in split:
        heights = jnp.exp(jax.random.uniform(jax.random.fold_in(own, position), (parts,), jnp.float32, smallest / len(split), high / len(split)))
        factor_of = factor_of * jnp.repeat(heights, dims[position] // parts).reshape([-1 if axis == position else 1 for axis in range(len(dims))])
    return factor_of


def assign_block(rng, own, number, rows, count, top, reach, slope):
    order = jax.random.permutation(rng, count)
    crowded, ordinary = portions_of(count, rows * top, reach, slope, True), portions_of(count, rows * top, reach, slope, False)
    places = jnp.arange(count)

    def named(lengths, offset_by):
        used = int((lengths > 0).sum())
        fixed = max(1, used // 4)
        shifted = fixed + (places - fixed + offset_by * (used - fixed)) % max(1, count - fixed)
        return jnp.zeros((count,), jnp.int32).at[order[jnp.where(places < fixed, places, shifted)]].set(jnp.asarray(lengths, jnp.int32))

    lengths = jnp.where(number % 4 == 0, named(crowded, number // 4), named(ordinary, number - number // 4 - 1))
    mixed = jax.random.permutation(jax.random.fold_in(own, 3), count)
    source_of, taker = mixed[0:count // 2 * 2:2], mixed[1:count // 2 * 2:2]
    margin = jnp.minimum(lengths[source_of] - 1, reach - lengths[taker]) // 2
    margin = jnp.where((source_of == order[0]) | (taker == order[0]) | (lengths[taker] == 0), 0, jnp.maximum(margin, 0))
    shifted = jax.random.randint(jax.random.fold_in(own, 4), (count // 2,), 0, 1 << 20) % (margin + 1)
    lengths = lengths.at[source_of].add(-shifted).at[taker].add(shifted)
    labels = jnp.searchsorted(jnp.cumsum(lengths), jnp.arange(rows * top), side="right").astype(jnp.int32)
    grid = labels.reshape(top, rows).T
    grid = grid[jax.random.permutation(jax.random.fold_in(own, 1), rows)]
    offset_by = jax.random.randint(jax.random.fold_in(own, 2), (rows, 1), 0, top)
    return jnp.take_along_axis(grid, (jnp.arange(top)[None, :] + offset_by) % top, axis=1)


def portions_of(number_of, total, bound, skew, full):
    weights = [(1 << 20) // math.isqrt(rank ** skew) + 1 for rank in range(1, number_of + 1)]
    largest = bound if full else min(bound, max(-(-total // number_of), total * weights[0] // sum(weights)))
    least = 1 if total - largest >= number_of - 1 else 0
    given, surplus = [largest] + [least] * (number_of - 1), total - largest - least * (number_of - 1)
    while surplus > 0:
        candidates = [i for i in range(1, number_of) if given[i] < largest] or [i for i in range(1, number_of) if given[i] < bound]
        mass, left = sum([weights[i] for i in candidates]), surplus
        for i in candidates:
            extra = min(bound - given[i], max(1, left * weights[i] // mass), surplus)
            given[i] = given[i] + extra
            surplus = surplus - extra
    return np.array(given)


def noise(key, shape, spread, reach, pieces=(), held_as=jnp.bfloat16):
    loudness = level_of(key, shape, pieces, -0.22, 0.18) if pieces else 1.0
    array = jax.random.normal(key, shape, jnp.float32) * spread * loudness
    return jnp.minimum(jnp.maximum(array, -reach), reach).astype(held_as)


def setup_inputs(seed: int = 0) -> dict:
    splits = jax.random.split(jax.random.key(seed), 7)
    tokens = noise(splits[0], (TOKENS, D), 1.0, 6.0, ((0, 16),))
    routes_keys = jax.random.split(jax.random.fold_in(splits[1], 1), TOKENS // TOK_DEV)
    routes_turns = jax.random.permutation(jax.random.fold_in(splits[1], 3), TOKENS // TOK_DEV)
    routes = jax.vmap(lambda own, number: assign_block(jax.random.fold_in(splits[1], 2), own, number, TOK_DEV, EXPERTS, 2, MOST, 2))(routes_keys, routes_turns).reshape((TOKENS, 2))
    combine = jnp.clip(0.25 + 0.75 * jax.random.uniform(splits[2], (TOKENS, 2), jnp.float32) ** level_of(splits[2], (TOKENS, 2), ((0, 16),), -0.2, 0.2), 0.25, 1.0)
    gate_weight = noise(splits[3], (EXPERTS, FF, D), D ** -0.5, 0.09375, ((0, 8), (2, 16)))
    up_weight = noise(splits[4], (EXPERTS, FF, D), D ** -0.5, 0.09375, ((0, 8), (2, 16)))
    down_weight = noise(splits[5], (EXPERTS, FF, D), FF ** -0.5, 0.0546875, ((0, 8), (2, 16)))
    return dict(tokens=tokens, routes=routes, combine=combine, gate_weight=gate_weight, up_weight=up_weight, down_weight=down_weight)


def reference(tokens, routes, combine, gate_weight, up_weight, down_weight):
    slot_total = N_FSDP * MOST

    def expert_pass(carry, expert):
        picked = routes == expert
        chosen = jnp.any(picked, axis=1)
        token_weight = jnp.sum(jnp.where(picked, combine, jnp.zeros_like(combine)), axis=1)
        index = jnp.nonzero(chosen, size=slot_total, fill_value=0)[0].astype(jnp.int32)
        valid = jnp.arange(slot_total, dtype=jnp.int32) < jnp.sum(chosen.astype(jnp.int32))
        rows = tokens[index]
        gate = jnp.dot(rows, gate_weight[expert].T, preferred_element_type=jnp.float32)
        upper = jnp.dot(rows, up_weight[expert].T, preferred_element_type=jnp.float32)
        hidden = (jax.nn.silu(gate) * upper).astype(jnp.bfloat16)
        output = jnp.dot(hidden, down_weight[expert], preferred_element_type=jnp.float32)
        scale = jnp.where(valid, token_weight[index], jnp.zeros_like(token_weight[index]))
        carry = carry.at[index].add(scale[:, None] * output)
        return carry, None

    start_sum = jnp.zeros((tokens.shape[0], tokens.shape[1]), jnp.float32)
    total, unused = lax.scan(expert_pass, start_sum, jnp.arange(EXPERTS, dtype=jnp.int32))
    return total.astype(jnp.bfloat16)
```

```python
import jax
import jax.numpy as jnp
from jax import lax
from jax.experimental import pallas as pl
from jax.experimental.pallas import tpu as pltpu
from jax.sharding import PartitionSpec as P

PIECE = 256
AHEAD = 3
MESH = pl.DeviceIdType.MESH


def contract(a, b, dims):
    return lax.dot_general(a, b, (dims, ((), ())), preferred_element_type=jnp.float32)


def kernel(
    packed, gate, up, down, out,
    tokbuf, tok, acc, wgu, wd, ps, pr, own, hb, osb, orv, fin, frv,
    tok_s, tok_r, gu_s, gu_r, d_s, d_r, p_s, p_r, h_s, h_r, o_s, o_r, f_s, f_r,
):
    steps = wgu.shape[0]
    slots = packed.shape[0]
    wide = tok.shape[1]
    group = tok.shape[0] // 4
    half = out.shape[2]
    me = lax.axis_index("member")
    shard = lax.axis_index("fsdp")
    z, x = shard // 4, shard % 4

    def first_row(xt):
        return xt * (steps * PIECE) - (xt // 3) * (4 * steps * PIECE - gate.shape[0])

    def wait(ref, sem):
        pltpu.make_async_copy(ref, ref, sem).wait()

    def columns(zt):
        return packed.at[:, pl.ds(pl.multiple_of(zt * wide, wide), wide)]

    def send_gate_up(c):
        for dx in (2, 1, 3):
            xt = (x + dx) % 4
            rows = pl.ds(pl.multiple_of(first_row(xt) + c * PIECE, PIECE), PIECE)
            for w, ref in enumerate((gate, up)):
                pltpu.make_async_remote_copy(
                    ref.at[rows], wgu.at[c, x, w], gu_s.at[c], gu_r.at[c],
                    device_id={"fsdp": z * 4 + xt}, device_id_type=MESH,
                ).start()
        rows = pl.ds(pl.multiple_of(first_row(x) + c * PIECE, PIECE), PIECE)
        for w, ref in enumerate((gate, up)):
            pltpu.make_async_copy(ref.at[rows], wgu.at[c, x, w], gu_r.at[c]).start()

    def send_down(c):
        for dx in (2, 1, 3):
            xt = (x + dx) % 4
            rows = pl.ds(pl.multiple_of(first_row(xt) + c * PIECE, PIECE), PIECE)
            pltpu.make_async_remote_copy(
                down.at[rows], wd.at[c, x], d_s.at[c], d_r.at[c],
                device_id={"fsdp": z * 4 + xt}, device_id_type=MESH,
            ).start()
        rows = pl.ds(pl.multiple_of(first_row(x) + c * PIECE, PIECE), PIECE)
        pltpu.make_async_copy(down.at[rows], wd.at[c, x], d_r.at[c]).start()

    for hop in range(1, 16):
        other = (shard + hop) % 16
        pltpu.make_async_remote_copy(
            columns(other // 4), tokbuf.at[shard], tok_s.at[hop], tok_r.at[shard],
            device_id={"fsdp": other}, device_id_type=MESH,
        ).start()
    pltpu.make_async_copy(columns(z), tokbuf.at[shard], tok_r.at[shard]).start()
    for c in range(AHEAD):
        send_gate_up(c)

    for f in range(16):
        wait(tokbuf.at[f], tok_r.at[f])
        acc[pl.ds(f * slots, slots), :] = tokbuf[f].astype(jnp.float32)
    for g in range(4):
        rows = pl.ds(g * group, group)
        tok[rows, :] = acc[rows, :].astype(tok.dtype)
    acc[...] = jnp.zeros_like(acc)

    def partial_sums(i):
        slot = i % 4
        wait(wgu.at[i], gu_r.at[i])

        @pl.when(i >= 4)
        def _():
            wait(ps.at[slot], p_s.at[i - 4])

        for dz in (2, 1, 3, 0):
            zt = (z + dz) % 4
            rows = pl.ds(pl.multiple_of(zt * group, 16), group)
            for w in range(2):
                total = contract(tok[rows, 0:PIECE], wgu[i, 0, w], ((1,), (1,)))
                for k in range(1, 4):
                    total += contract(
                        tok[rows, k * PIECE : (k + 1) * PIECE], wgu[i, k, w], ((1,), (1,))
                    )
                if dz:
                    ps[slot, dz - 1, w] = total.astype(ps.dtype)
                else:
                    own[i % 2, w] = total
            if dz:
                pltpu.make_async_remote_copy(
                    ps.at[slot, dz - 1], pr.at[i, dz - 1], p_s.at[i], p_r.at[i],
                    device_id={"fsdp": zt * 4 + x}, device_id_type=MESH,
                ).start()

    def activate(j):
        wait(pr.at[j], p_r.at[j])
        sums = []
        for w in range(2):
            total = own[j % 2, w]
            for s in range(3):
                total += pr[j, s, w].astype(jnp.float32)
            sums.append(total)
        hidden = sums[0] / (1.0 + jnp.exp(-sums[0])) * sums[1]
        twice = jnp.logical_and(x == 3, j * PIECE < 4 * steps * PIECE - gate.shape[0])
        hidden = jnp.where(twice, jnp.zeros_like(hidden), hidden)
        hb[j, z] = hidden.astype(hb.dtype)
        for dz in (2, 1, 3):
            pltpu.make_async_remote_copy(
                hb.at[j, z], hb.at[j, z], h_s.at[j], h_r.at[j],
                device_id={"fsdp": ((z + dz) % 4) * 4 + x}, device_id_type=MESH,
            ).start()

    def project(k):
        wait(hb.at[k, 0:3], h_r.at[k])
        wait(wd.at[k], d_r.at[k])
        for g in range(4):
            rows = pl.ds(g * group, group)
            for b in range(4):
                cols = slice(b * PIECE, (b + 1) * PIECE)
                acc[rows, cols] += contract(hb[k, g], wd[k, b], ((1,), (0,)))

    def step(i, carry):
        @pl.when(i + AHEAD < steps)
        def _():
            send_gate_up(i + AHEAD)

        @pl.when(i < steps)
        def _():
            send_down(i)
            partial_sums(i)

        @pl.when(jnp.logical_and(i >= 1, i < steps + 1))
        def _():
            activate(i - 1)

        @pl.when(i >= 2)
        def _():
            project(i - 2)

        return carry

    lax.fori_loop(0, steps + 2, step, 0)

    for dx in (2, 1, 3):
        xt = (x + dx) % 4
        for zb in range(4):
            rows = pl.ds(pl.multiple_of((zb * 4 + xt) * slots, 8), slots)
            osb[dx - 1, zb] = acc[rows, :].astype(osb.dtype)
        pltpu.make_async_remote_copy(
            osb.at[dx - 1], orv.at[dx - 1], o_s.at[dx - 1], o_r.at[dx - 1],
            device_id={"fsdp": z * 4 + xt}, device_id_type=MESH,
        ).start()
    for s in range(3):
        wait(orv.at[s], o_r.at[s])
    for zb in range(4):
        rows = pl.ds(pl.multiple_of((zb * 4 + x) * slots, 8), slots)
        total = acc[rows, :]
        for s in range(3):
            total += orv[s, zb].astype(jnp.float32)
        for h in range(2):
            fin[zb, h] = total[:, h * half : (h + 1) * half].astype(fin.dtype)
    for zb in range(4):
        for h in range(2):
            here = jnp.logical_and(me == 2 * z + h, zb == z)

            @pl.when(jnp.logical_not(here))
            def _():
                copy = pltpu.make_async_remote_copy(
                    fin.at[zb, h], frv.at[me], f_s.at[zb * 2 + h], f_r.at[me],
                    device_id={"member": 2 * z + h, "fsdp": zb * 4 + x}, device_id_type=MESH,
                )
                copy.start()

            @pl.when(here)
            def _():
                pltpu.make_async_copy(fin.at[zb, h], frv.at[me], f_r.at[me]).start()

    for m in range(8):
        wait(frv.at[m], f_r.at[m])
        out[m] = frv[m]

    for zb in range(4):
        for h in range(2):
            @pl.when(jnp.logical_not(jnp.logical_and(me == 2 * z + h, zb == z)))
            def _():
                wait(fin.at[zb, h], f_s.at[zb * 2 + h])

    for s in range(3):
        wait(osb.at[s], o_s.at[s])
    for hop in range(1, 16):
        wait(tokbuf.at[0], tok_s.at[hop])

    def finish(c, carry):
        wait(wgu.at[c, 0:3], gu_s.at[c])
        wait(wd.at[c, 0:3], d_s.at[c])
        wait(hb.at[c, 0:3], h_s.at[c])

        @pl.when(c >= steps - 4)
        def _():
            wait(ps.at[c % 4], p_s.at[c])

        return carry

    lax.fori_loop(0, steps, finish, 0)


def exchange(packed, gate, up, down):
    slots, wide = packed.shape[0], packed.shape[1] // 4
    rows = 16 * slots
    steps = -(-gate.shape[0] // (4 * PIECE))
    half = packed.shape[1] // 8
    bf16, f32 = jnp.bfloat16, jnp.float32
    dma = pltpu.SemaphoreType.DMA
    return pl.pallas_call(
        kernel,
        out_shape=jax.ShapeDtypeStruct((8, slots, half), bf16),
        in_specs=[pl.BlockSpec(memory_space=pl.ANY)] * 4,
        out_specs=pl.BlockSpec(memory_space=pltpu.VMEM),
        scratch_shapes=[
            pltpu.VMEM((16, slots, wide), bf16),
            pltpu.VMEM((rows, wide), bf16),
            pltpu.VMEM((rows, wide), f32),
            pltpu.VMEM((steps, 4, 2, PIECE, PIECE), bf16),
            pltpu.VMEM((steps, 4, PIECE, PIECE), bf16),
            pltpu.VMEM((4, 3, 2, rows // 4, PIECE), bf16),
            pltpu.VMEM((steps, 3, 2, rows // 4, PIECE), bf16),
            pltpu.VMEM((2, 2, rows // 4, PIECE), f32),
            pltpu.VMEM((steps, 4, rows // 4, PIECE), bf16),
            pltpu.VMEM((3, 4, slots, wide), bf16),
            pltpu.VMEM((3, 4, slots, wide), bf16),
            pltpu.VMEM((4, 2, slots, half), bf16),
            pltpu.VMEM((8, slots, half), bf16),
            dma((16,)), dma((16,)),
            dma((steps,)), dma((steps,)), dma((steps,)), dma((steps,)),
            dma((steps,)), dma((steps,)), dma((steps,)), dma((steps,)),
            dma((3,)), dma((3,)), dma((8,)), dma((8,)),
        ],
        compiler_params=pltpu.CompilerParams(
            has_side_effects=True, vmem_limit_bytes=67043328
        ),
    )(packed, gate, up, down)


def body(tokens, routes, combine, gate_weight, up_weight, down_weight):
    expert = lax.axis_index("member")
    experts = lax.axis_size("member")
    slots = 3 * tokens.shape[0] // experts
    ids = jnp.arange(experts, dtype=routes.dtype)
    named = routes[:, :, None] == ids[None, None, :]
    chosen = jnp.any(named, axis=1)
    order = jnp.cumsum(chosen.astype(jnp.int32), axis=0) - 1
    slot_ids = jnp.arange(slots, dtype=jnp.int32)
    mine = jnp.any(routes == expert, axis=1)
    position = jnp.sum(jnp.where(ids[None, :] == expert, order, 0), axis=1)
    placed = (position[:, None] == slot_ids[None, :]) & mine[:, None]
    packed = lax.dot_general(
        placed.astype(jnp.bfloat16), tokens, (((0,), (0,)), ((), ())),
        preferred_element_type=jnp.float32,
    ).astype(jnp.bfloat16)
    parts = exchange(packed, gate_weight[0], up_weight[0], down_weight[0])
    place = jnp.sum(jnp.where(named, (order + ids[None, :] * slots)[:, None, :], 0), axis=2)
    rows = parts.reshape(experts * slots, parts.shape[2])
    all_ids = jnp.arange(experts * slots, dtype=jnp.int32)
    mixed = 0.0
    for k in range(routes.shape[1]):
        pick = (place[:, k][:, None] == all_ids[None, :]).astype(jnp.bfloat16)
        mixed += combine[:, k][:, None] * jnp.dot(
            pick, rows, preferred_element_type=jnp.float32
        )
    return mixed.astype(jnp.bfloat16)


def solution(mesh):
    placed = (
        P("fsdp", None),
        P("fsdp", None),
        P("fsdp", None),
        P("member", None, "fsdp"),
        P("member", None, "fsdp"),
        P("member", None, "fsdp"),
    )
    return jax.shard_map(
        body, mesh=mesh, in_specs=placed, out_specs=P("fsdp", "member"), check_vma=False
    )
```

```python
import jax
import jax.numpy as jnp
from jax import lax
from jax.experimental import pallas as pl
from jax.experimental.pallas import tpu as pltpu
from jax.sharding import PartitionSpec as P

PIECE = 256
AHEAD = 3
MESH = pl.DeviceIdType.MESH


def contract(a, b, dims):
    return lax.dot_general(a, b, (dims, ((), ())), preferred_element_type=jnp.float32)


def kernel(
    tokens, routes, combine, gate, up, down, out,
    tokv, packed, tokbuf, tok, acc, wgu, wd, ps, rl, pr, own, keep, hb, osb, orv, fin, frv,
    t_c, tok_s, tok_r, gu_s, gu_r, d_s, d_r, p_s, l_r, p_r, h_s, h_r, o_s, o_r, f_s, f_r,
):
    steps = wgu.shape[0]
    slots = packed.shape[0]
    wide = tok.shape[1]
    group = tok.shape[0] // 4
    half = out.shape[1]
    count = tokv.shape[0]
    me = lax.axis_index("member")
    shard = lax.axis_index("fsdp")
    z, x = shard // 4, shard % 4

    def first_row(xt):
        return xt * (steps * PIECE) - (xt // 3) * (4 * steps * PIECE - gate.shape[0])

    def wait(ref, sem):
        pltpu.make_async_copy(ref, ref, sem).wait()

    def remote(src, dst, send, recv, zt, xt):
        pltpu.make_async_remote_copy(
            src, dst, send, recv, device_id={"fsdp": zt * 4 + xt}, device_id_type=MESH
        ).start()

    def columns(zt):
        return packed.at[:, pl.ds(pl.multiple_of(zt * wide, wide), wide)]

    def send_gate_up(c):
        for dx in (2, 1, 3):
            xt = (x + dx) % 4
            rows = pl.ds(pl.multiple_of(first_row(xt) + c * PIECE, PIECE), PIECE)
            for w, ref in enumerate((gate, up)):
                remote(ref.at[rows], wgu.at[c, x, w], gu_s.at[c], gu_r.at[c], z, xt)
        rows = pl.ds(pl.multiple_of(first_row(x) + c * PIECE, PIECE), PIECE)
        for w, ref in enumerate((gate, up)):
            pltpu.make_async_copy(ref.at[rows], wgu.at[c, x, w], gu_r.at[c]).start()

    def send_down(c):
        for dx in (2, 1, 3):
            xt = (x + dx) % 4
            rows = pl.ds(pl.multiple_of(first_row(xt) + c * PIECE, PIECE), PIECE)
            remote(down.at[rows], wd.at[c, x], d_s.at[c], d_r.at[c], z, xt)
        rows = pl.ds(pl.multiple_of(first_row(x) + c * PIECE, PIECE), PIECE)
        pltpu.make_async_copy(down.at[rows], wd.at[c, x], d_r.at[c]).start()

    load = pltpu.make_async_copy(tokens, tokv, t_c)
    load.start()
    send_gate_up(0)

    lanes = lax.broadcasted_iota(jnp.int32, (count, 128), 1)
    earlier = lax.broadcasted_iota(jnp.int32, (count, count), 0) >= (
        lax.broadcasted_iota(jnp.int32, (count, count), 1)
    )
    named = jnp.logical_or(routes[:, 0:1] == lanes, routes[:, 1:2] == lanes)
    order = contract(
        earlier.astype(jnp.bfloat16), named.astype(jnp.bfloat16), ((1,), (0,))
    ).astype(jnp.int32)
    mine = jnp.sum(jnp.where(jnp.logical_and(named, lanes == me), order, 0), axis=1, keepdims=True)
    placed = jnp.where(mine - 1 == lanes, 1.0, 0.0).T[0:slots].astype(jnp.bfloat16)
    load.wait()
    for q in range(4):
        cols = slice(q * wide, (q + 1) * wide)
        packed[:, cols] = contract(placed, tokv[:, cols], ((1,), (0,))).astype(packed.dtype)

    for hop in range(1, 16):
        other = (shard + hop) % 16
        remote(
            columns(other // 4), tokbuf.at[shard], tok_s.at[hop], tok_r.at[shard],
            other // 4, other % 4,
        )
    pltpu.make_async_copy(columns(z), tokbuf.at[shard], tok_r.at[shard]).start()
    for c in range(1, AHEAD):
        send_gate_up(c)

    for f in range(16):
        wait(tokbuf.at[f], tok_r.at[f])
        acc[pl.ds(f * slots, slots), :] = tokbuf[f].astype(jnp.float32)
    for g in range(4):
        rows = pl.ds(g * group, group)
        tok[rows, :] = acc[rows, :].astype(tok.dtype)
    acc[...] = jnp.zeros_like(acc)

    def partial_sums(i):
        slot = i % 4
        wait(wgu.at[i], gu_r.at[i])

        @pl.when(i >= 4)
        def _():
            wait(ps.at[slot], p_s.at[i - 4])

        def share(dz, w):
            rows = pl.ds(pl.multiple_of(((z + dz) % 4) * group, 16), group)
            total = contract(tok[rows, 0:PIECE], wgu[i, 0, w], ((1,), (1,)))
            for k in range(1, 4):
                total += contract(
                    tok[rows, k * PIECE : (k + 1) * PIECE], wgu[i, k, w], ((1,), (1,))
                )
            return total

        def emit(n, dz, w, dst, sem, to):
            ps[slot, n] = share(dz, w).astype(ps.dtype)
            remote(ps.at[slot, n], dst, p_s.at[i], sem, (z + to) % 4, x)

        emit(0, 2, 0, rl.at[i, 0], l_r.at[i], 1)
        emit(1, 2, 1, rl.at[i, 1], l_r.at[i], 3)
        emit(2, 1, 1, pr.at[i, 0], p_r.at[i], 1)
        emit(3, 3, 0, pr.at[i, 1], p_r.at[i], 3)
        keep[i % 2, 0] = share(1, 0)
        keep[i % 2, 1] = share(3, 1)
        own[i % 4, 0] = share(0, 0)
        own[i % 4, 1] = share(0, 1)

    def merge(j):
        wait(rl.at[j], l_r.at[j])
        for w, to in ((0, 1), (1, 3)):
            total = keep[j % 2, w] + rl[j, w].astype(jnp.float32)
            ps[j % 4, 4 + w] = total.astype(ps.dtype)
            remote(ps.at[j % 4, 4 + w], pr.at[j, 2 + w], p_s.at[j], p_r.at[j], (z + to) % 4, x)

    def activate(j):
        wait(pr.at[j], p_r.at[j])
        sums = [
            own[j % 4, w] + pr[j, 1 - w].astype(jnp.float32) + pr[j, 2 + w].astype(jnp.float32)
            for w in range(2)
        ]
        hidden = sums[0] / (1.0 + jnp.exp(-sums[0])) * sums[1]
        twice = jnp.logical_and(x == 3, j * PIECE < 4 * steps * PIECE - gate.shape[0])
        hidden = jnp.where(twice, jnp.zeros_like(hidden), hidden)
        hb[j, z] = hidden.astype(hb.dtype)
        for dz in (2, 1, 3):
            remote(hb.at[j, z], hb.at[j, z], h_s.at[j], h_r.at[j], (z + dz) % 4, x)

    def project(k):
        wait(hb.at[k, 0:3], h_r.at[k])
        wait(wd.at[k], d_r.at[k])
        for g in range(4):
            rows = pl.ds(g * group, group)
            for b in range(4):
                cols = slice(b * PIECE, (b + 1) * PIECE)
                acc[rows, cols] += contract(hb[k, g], wd[k, b], ((1,), (0,)))

    def step(i, carry):
        @pl.when(i + AHEAD < steps)
        def _():
            send_gate_up(i + AHEAD)

        @pl.when(i < steps)
        def _():
            send_down(i)
            partial_sums(i)

        @pl.when(jnp.logical_and(i >= 1, i < steps + 1))
        def _():
            merge(i - 1)

        @pl.when(jnp.logical_and(i >= 2, i < steps + 2))
        def _():
            activate(i - 2)

        @pl.when(i >= 3)
        def _():
            project(i - 3)

        return carry

    lax.fori_loop(0, steps + 3, step, 0)

    for dzb in (2, 1, 3, 0):
        zb = (z + dzb) % 4
        for dx in (2, 1, 3):
            xt = (x + dx) % 4
            rows = pl.ds(pl.multiple_of((zb * 4 + xt) * slots, 8), slots)
            osb[dzb, dx - 1] = acc[rows, :].astype(osb.dtype)
            remote(
                osb.at[dzb, dx - 1], orv.at[dzb, dx - 1],
                o_s.at[dzb * 3 + dx - 1], o_r.at[dzb * 3 + dx - 1], z, xt,
            )
    for dzb in (2, 1, 3, 0):
        zb = (z + dzb) % 4
        rows = pl.ds(pl.multiple_of((zb * 4 + x) * slots, 8), slots)
        total = acc[rows, :]
        for s in range(3):
            wait(orv.at[dzb, s], o_r.at[dzb * 3 + s])
            total += orv[dzb, s].astype(jnp.float32)
        for h in range(2):
            n = dzb * 2 + h
            fin[dzb, h] = total[:, h * half : (h + 1) * half].astype(fin.dtype)

            def leave(n=n, h=h, dzb=dzb, zb=zb):
                pltpu.make_async_remote_copy(
                    fin.at[dzb, h], frv.at[me], f_s.at[n], f_r.at[me],
                    device_id={"member": 2 * z + h, "fsdp": zb * 4 + x}, device_id_type=MESH,
                ).start()

            if dzb:
                leave()
            else:
                pl.when(me != 2 * z + h)(leave)

                @pl.when(me == 2 * z + h)
                def _():
                    pltpu.make_async_copy(fin.at[dzb, h], frv.at[me], f_r.at[me]).start()

    mixed = jnp.zeros((count, half), jnp.float32)
    for m in range(8):
        pick = jnp.where(
            jnp.logical_and(order[:, m : m + 1] - 1 == lanes, named[:, m : m + 1]), 1.0, 0.0
        )[:, 0:slots].astype(jnp.bfloat16)
        scale = jnp.sum(jnp.where(routes[...] == m, combine[...], 0.0), axis=1, keepdims=True)
        wait(frv.at[m], f_r.at[m])
        mixed += scale * contract(pick, frv[m], ((1,), (0,)))
    out[...] = mixed.astype(out.dtype)

    for dzb in range(4):
        for h in range(2):
            if dzb:
                wait(fin.at[dzb, h], f_s.at[dzb * 2 + h])
            else:
                @pl.when(me != 2 * z + h)
                def _():
                    wait(fin.at[dzb, h], f_s.at[dzb * 2 + h])
        for s in range(3):
            wait(osb.at[dzb, s], o_s.at[dzb * 3 + s])
    for hop in range(1, 16):
        wait(tokbuf.at[0], tok_s.at[hop])

    def finish(c, carry):
        wait(wgu.at[c, 0:3], gu_s.at[c])
        wait(wd.at[c, 0:3], d_s.at[c])
        wait(hb.at[c, 0:3], h_s.at[c])

        @pl.when(c >= steps - 4)
        def _():
            wait(ps.at[c % 4], p_s.at[c])

        return carry

    lax.fori_loop(0, steps, finish, 0)


def body(tokens, routes, combine, gate_weight, up_weight, down_weight):
    count, features = tokens.shape
    experts = lax.axis_size("member")
    gate, up, down = gate_weight[0], up_weight[0], down_weight[0]
    slots, wide, half = 3 * count // experts, features // 4, features // 8
    rows = 16 * slots
    steps = -(-gate.shape[0] // (4 * PIECE))
    bf16, f32 = jnp.bfloat16, jnp.float32
    dma = pltpu.SemaphoreType.DMA
    whole = pl.BlockSpec(memory_space=pltpu.VMEM)
    away = pl.BlockSpec(memory_space=pl.ANY)
    part = (rows // 4, PIECE)
    return pl.pallas_call(
        kernel,
        out_shape=jax.ShapeDtypeStruct((count, half), bf16),
        in_specs=[away, whole, whole, away, away, away],
        out_specs=whole,
        scratch_shapes=[
            pltpu.VMEM((count, features), bf16),
            pltpu.VMEM((slots, features), bf16),
            pltpu.VMEM((16, slots, wide), bf16),
            pltpu.VMEM((rows, wide), bf16),
            pltpu.VMEM((rows, wide), f32),
            pltpu.VMEM((steps, 4, 2, PIECE, PIECE), bf16),
            pltpu.VMEM((steps, 4, PIECE, PIECE), bf16),
            pltpu.VMEM((4, 6) + part, bf16),
            pltpu.VMEM((steps, 2) + part, bf16),
            pltpu.VMEM((steps, 4) + part, bf16),
            pltpu.VMEM((4, 2) + part, f32),
            pltpu.VMEM((2, 2) + part, f32),
            pltpu.VMEM((steps, 4) + part, bf16),
            pltpu.VMEM((4, 3, slots, wide), bf16),
            pltpu.VMEM((4, 3, slots, wide), bf16),
            pltpu.VMEM((4, 2, slots, half), bf16),
            pltpu.VMEM((8, slots, half), bf16),
            dma(()), dma((16,)), dma((16,)),
            dma((steps,)), dma((steps,)), dma((steps,)), dma((steps,)),
            dma((steps,)), dma((steps,)), dma((steps,)), dma((steps,)), dma((steps,)),
            dma((12,)), dma((12,)), dma((8,)), dma((8,)),
        ],
        compiler_params=pltpu.CompilerParams(
            has_side_effects=True, vmem_limit_bytes=67043328
        ),
    )(tokens, routes, combine, gate, up, down)


def solution(mesh):
    placed = (
        P("fsdp", None),
        P("fsdp", None),
        P("fsdp", None),
        P("member", None, "fsdp"),
        P("member", None, "fsdp"),
        P("member", None, "fsdp"),
    )
    return jax.shard_map(
        body, mesh=mesh, in_specs=placed, out_specs=P("fsdp", "member"), check_vma=False
    )
```

```python
import jax
import jax.numpy as jnp
from jax import lax
from jax.experimental import pallas as pl
from jax.experimental.pallas import tpu as pltpu
from jax.sharding import PartitionSpec as P

PIECE = 256
AHEAD = 3
MESH = pl.DeviceIdType.MESH


def contract(a, b, dims):
    return lax.dot_general(a, b, (dims, ((), ())), preferred_element_type=jnp.float32)


def kernel(
    tokens, routes, combine, gate, up, down, out,
    tokv, packed, tokbuf, tok, acc, wgu, wd, ps, rl, pr, own, keep, hb, osb, orv, fin, frv,
    t_c, tok_s, tok_r, gu_s, gu_r, d_s, d_r, p_s, l_r, p_r, h_s, h_r, q_s, q_r, o_s, o_r, f_s, f_r,
):
    steps = wgu.shape[0]
    slots = packed.shape[0]
    wide = tok.shape[1]
    group = tok.shape[0] // 4
    half = out.shape[1]
    count = tokv.shape[0]
    me = lax.axis_index("member")
    shard = lax.axis_index("fsdp")
    z, x = shard // 4, shard % 4

    share_rows = gate.shape[0] // 4
    short = share_rows - (steps - 1) * PIECE

    def span(xt, c):
        if isinstance(c, int) and c == 0:
            return pl.ds(pl.multiple_of(xt * share_rows, 64), short)
        return pl.ds(pl.multiple_of(xt * share_rows + short + (c - 1) * PIECE, 64), PIECE)

    def filled(ref, c):
        return ref.at[0:short] if isinstance(c, int) and c == 0 else ref

    def wait(ref, sem):
        pltpu.make_async_copy(ref, ref, sem).wait()

    def remote(src, dst, send, recv, zt, xt):
        pltpu.make_async_remote_copy(
            src, dst, send, recv, device_id={"fsdp": zt * 4 + xt}, device_id_type=MESH
        ).start()

    def columns(zt):
        return packed.at[:, pl.ds(pl.multiple_of(zt * wide, wide), wide)]

    def send_gate_up(c):
        for dx in (2, 1, 3):
            xt = (x + dx) % 4
            for w, ref in enumerate((gate, up)):
                remote(
                    ref.at[span(xt, c)], filled(wgu.at[c, x, w], c),
                    gu_s.at[c], gu_r.at[c], z, xt,
                )
        for w, ref in enumerate((gate, up)):
            pltpu.make_async_copy(
                ref.at[span(x, c)], filled(wgu.at[c, x, w], c), gu_r.at[c]
            ).start()

    def send_down(c):
        for dx in (2, 1, 3):
            xt = (x + dx) % 4
            remote(down.at[span(xt, c)], filled(wd.at[c, x], c), d_s.at[c], d_r.at[c], z, xt)
        pltpu.make_async_copy(down.at[span(x, c)], filled(wd.at[c, x], c), d_r.at[c]).start()

    barrier = pltpu.get_barrier_semaphore()
    for hop in range(1, 16):
        pl.semaphore_signal(
            barrier, inc=1, device_id={"fsdp": (shard + hop) % 16}, device_id_type=MESH
        )
    inside = me // 2 == z
    for m in range(8):
        @pl.when(jnp.logical_not(jnp.logical_and(inside, me == m)))
        def _():
            pl.semaphore_signal(
                barrier, inc=1, device_id={"member": m, "fsdp": (me // 2) * 4 + x},
                device_id_type=MESH,
            )

    load = pltpu.make_async_copy(tokens, tokv, t_c)
    load.start()
    wgu[0, :, :, short:, :] = jnp.zeros((4, 2, PIECE - short, PIECE), wgu.dtype)
    wd[0, :, short:, :] = jnp.zeros((4, PIECE - short, PIECE), wd.dtype)

    lanes = lax.broadcasted_iota(jnp.int32, (count, 128), 1)
    earlier = lax.broadcasted_iota(jnp.int32, (count, count), 0) >= (
        lax.broadcasted_iota(jnp.int32, (count, count), 1)
    )
    named = jnp.logical_or(routes[:, 0:1] == lanes, routes[:, 1:2] == lanes)
    order = contract(
        earlier.astype(jnp.bfloat16), named.astype(jnp.bfloat16), ((1,), (0,))
    ).astype(jnp.int32)
    mine = jnp.sum(jnp.where(jnp.logical_and(named, lanes == me), order, 0), axis=1, keepdims=True)
    placed = jnp.where(mine - 1 == lanes, 1.0, 0.0).T[0:slots].astype(jnp.bfloat16)
    load.wait()
    for q in range(4):
        cols = slice(q * wide, (q + 1) * wide)
        packed[:, cols] = contract(placed, tokv[:, cols], ((1,), (0,))).astype(packed.dtype)

    @pl.when(inside)
    def _():
        pl.semaphore_wait(barrier, 22)

    @pl.when(jnp.logical_not(inside))
    def _():
        pl.semaphore_wait(barrier, 23)

    def spread(dz):
        zt = (z + dz) % 4
        for dx in (2, 1, 3, 0):
            xt = (x + dx) % 4
            if dz or dx:
                remote(
                    columns(zt), tokbuf.at[shard], tok_s.at[dz * 4 + dx], tok_r.at[shard], zt, xt
                )
            else:
                pltpu.make_async_copy(columns(z), tokbuf.at[shard], tok_r.at[shard]).start()

    spread(2)
    send_gate_up(0)
    for dz in (1, 3, 0):
        spread(dz)
    for c in range(1, AHEAD + 1):
        send_gate_up(c)
    send_down(0)

    def unpack(dz):
        zt = (z + dz) % 4
        for k in range(4):
            f = zt * 4 + k
            wait(tokbuf.at[f], tok_r.at[f])
            acc[pl.ds(pl.multiple_of(f * slots, 8), slots), :] = tokbuf[f].astype(jnp.float32)
        rows = pl.ds(pl.multiple_of(zt * group, 16), group)
        tok[rows, :] = acc[rows, :].astype(tok.dtype)

    def partial_sums(i):
        slot = i % 4
        first = isinstance(i, int)
        ready = (lambda dz: unpack(dz)) if first else (lambda dz: None)
        if first:
            ready(2)
            wait(wgu.at[0, :, :, 0:short], gu_r.at[0])
        else:
            wait(wgu.at[i], gu_r.at[i])

            @pl.when(i >= 4)
            def _():
                wait(ps.at[slot], p_s.at[i - 4])

        def share(dz, w):
            rows = pl.ds(pl.multiple_of(((z + dz) % 4) * group, 16), group)
            total = contract(tok[rows, 0:PIECE], wgu[i, 0, w], ((1,), (1,)))
            for k in range(1, 4):
                total += contract(
                    tok[rows, k * PIECE : (k + 1) * PIECE], wgu[i, k, w], ((1,), (1,))
                )
            return total

        def emit(n, dz, w, dst, sem, to):
            ps[slot, n] = share(dz, w).astype(ps.dtype)
            remote(ps.at[slot, n], dst, p_s.at[i], sem, (z + to) % 4, x)

        emit(0, 2, 0, rl.at[i, 0], l_r.at[i], 1)
        emit(1, 2, 1, rl.at[i, 1], l_r.at[i], 3)
        ready(1)
        emit(2, 1, 1, pr.at[i, 0], p_r.at[i], 1)
        ready(3)
        emit(3, 3, 0, pr.at[i, 1], p_r.at[i], 3)
        ready(0)
        keep[i % 2, 0] = share(1, 0)
        keep[i % 2, 1] = share(3, 1)
        own[i % 4, 0] = share(0, 0)
        own[i % 4, 1] = share(0, 1)

    def merge(j):
        wait(rl.at[j], l_r.at[j])
        for w, to in ((0, 1), (1, 3)):
            total = keep[j % 2, w] + rl[j, w].astype(jnp.float32)
            ps[j % 4, 4 + w] = total.astype(ps.dtype)
            remote(ps.at[j % 4, 4 + w], pr.at[j, 2 + w], p_s.at[j], p_r.at[j], (z + to) % 4, x)

    def activate(j):
        wait(pr.at[j], p_r.at[j])
        sums = [
            own[j % 4, w] + pr[j, 1 - w].astype(jnp.float32) + pr[j, 2 + w].astype(jnp.float32)
            for w in range(2)
        ]
        hidden = sums[0] / (1.0 + jnp.exp(-sums[0])) * sums[1]
        hb[j, z] = hidden.astype(hb.dtype)
        for dz in (1, 3):
            remote(hb.at[j, z], hb.at[j, z], h_s.at[j], h_r.at[j], (z + dz) % 4, x)

    def forward(j):
        wait(hb.at[j, 0:2], h_r.at[j])
        for dz, lo in ((1, 0), (3, group // 2)):
            piece = hb.at[j, (z - dz + 4) % 4, pl.ds(lo, group // 2)]
            remote(piece, piece, q_s.at[j], q_r.at[j], (z + dz) % 4, x)

    def project(k):
        wait(hb.at[k, 0], q_r.at[k])

        @pl.when(k == 0)
        def _():
            wait(wd.at[0, :, 0:short], d_r.at[0])

        @pl.when(k > 0)
        def _():
            wait(wd.at[k], d_r.at[k])

        for g in range(4):
            rows = pl.ds(g * group, group)
            for b in range(4):
                cols = slice(b * PIECE, (b + 1) * PIECE)
                acc[rows, cols] += contract(hb[k, g], wd[k, b], ((1,), (0,)))

    def step(i, carry):
        @pl.when(i + AHEAD < steps)
        def _():
            send_gate_up(i + AHEAD)

        @pl.when(i < steps)
        def _():
            send_down(i)
            partial_sums(i)

        @pl.when(i < steps + 1)
        def _():
            merge(i - 1)

        @pl.when(jnp.logical_and(i >= 2, i < steps + 2))
        def _():
            activate(i - 2)

        @pl.when(jnp.logical_and(i >= 3, i < steps + 3))
        def _():
            forward(i - 3)

        @pl.when(i >= 4)
        def _():
            project(i - 4)

        return carry

    partial_sums(0)
    acc[...] = jnp.zeros_like(acc)
    lax.fori_loop(1, steps + 4, step, 0)

    for dzb in (2, 1, 3, 0):
        zb = (z + dzb) % 4
        for dx in (2, 1, 3):
            xt = (x + dx) % 4
            rows = pl.ds(pl.multiple_of((zb * 4 + xt) * slots, 8), slots)
            osb[dzb, dx - 1] = acc[rows, :].astype(osb.dtype)
            remote(
                osb.at[dzb, dx - 1], orv.at[dzb, dx - 1],
                o_s.at[dzb * 3 + dx - 1], o_r.at[dzb * 3 + dx - 1], z, xt,
            )
    for dzb in (2, 1, 3, 0):
        zb = (z + dzb) % 4
        rows = pl.ds(pl.multiple_of((zb * 4 + x) * slots, 8), slots)
        total = acc[rows, :]
        for s in range(3):
            wait(orv.at[dzb, s], o_r.at[dzb * 3 + s])
            total += orv[dzb, s].astype(jnp.float32)
        for h in range(2):
            n = dzb * 2 + h
            fin[dzb, h] = total[:, h * half : (h + 1) * half].astype(fin.dtype)

            def leave(n=n, h=h, dzb=dzb, zb=zb):
                pltpu.make_async_remote_copy(
                    fin.at[dzb, h], frv.at[me], f_s.at[n], f_r.at[me],
                    device_id={"member": 2 * z + h, "fsdp": zb * 4 + x}, device_id_type=MESH,
                ).start()

            if dzb:
                leave()
            else:
                pl.when(me != 2 * z + h)(leave)

                @pl.when(me == 2 * z + h)
                def _():
                    pltpu.make_async_copy(fin.at[dzb, h], frv.at[me], f_r.at[me]).start()

    mixed = jnp.zeros((count, half), jnp.float32)
    for m in range(8):
        pick = jnp.where(
            jnp.logical_and(order[:, m : m + 1] - 1 == lanes, named[:, m : m + 1]), 1.0, 0.0
        )[:, 0:slots].astype(jnp.bfloat16)
        scale = jnp.sum(jnp.where(routes[...] == m, combine[...], 0.0), axis=1, keepdims=True)
        wait(frv.at[m], f_r.at[m])
        mixed += scale * contract(pick, frv[m], ((1,), (0,)))
    out[...] = mixed.astype(out.dtype)

    for dzb in range(4):
        for h in range(2):
            if dzb:
                wait(fin.at[dzb, h], f_s.at[dzb * 2 + h])
            else:
                @pl.when(me != 2 * z + h)
                def _():
                    wait(fin.at[dzb, h], f_s.at[dzb * 2 + h])
        for s in range(3):
            wait(osb.at[dzb, s], o_s.at[dzb * 3 + s])
    for hop in range(1, 16):
        wait(tokbuf.at[0], tok_s.at[hop])
    wait(wgu.at[0, 0:3, :, 0:short], gu_s.at[0])
    wait(wd.at[0, 0:3, 0:short], d_s.at[0])

    def finish(c, carry):
        @pl.when(c >= 1)
        def _():
            wait(wgu.at[c, 0:3], gu_s.at[c])
            wait(wd.at[c, 0:3], d_s.at[c])

        wait(hb.at[c, 0:2], h_s.at[c])
        wait(hb.at[c, 0], q_s.at[c])

        @pl.when(c >= steps - 4)
        def _():
            wait(ps.at[c % 4], p_s.at[c])

        return carry

    lax.fori_loop(0, steps, finish, 0)


def body(tokens, routes, combine, gate_weight, up_weight, down_weight):
    count, features = tokens.shape
    experts = lax.axis_size("member")
    gate, up, down = gate_weight[0], up_weight[0], down_weight[0]
    slots, wide, half = 3 * count // experts, features // 4, features // 8
    rows = 16 * slots
    steps = -(-gate.shape[0] // (4 * PIECE))
    bf16, f32 = jnp.bfloat16, jnp.float32
    dma = pltpu.SemaphoreType.DMA
    whole = pl.BlockSpec(memory_space=pltpu.VMEM)
    away = pl.BlockSpec(memory_space=pl.ANY)
    part = (rows // 4, PIECE)
    return pl.pallas_call(
        kernel,
        out_shape=jax.ShapeDtypeStruct((count, half), bf16),
        in_specs=[away, whole, whole, away, away, away],
        out_specs=whole,
        scratch_shapes=[
            pltpu.VMEM((count, features), bf16),
            pltpu.VMEM((slots, features), bf16),
            pltpu.VMEM((16, slots, wide), bf16),
            pltpu.VMEM((rows, wide), bf16),
            pltpu.VMEM((rows, wide), f32),
            pltpu.VMEM((steps, 4, 2, PIECE, PIECE), bf16),
            pltpu.VMEM((steps, 4, PIECE, PIECE), bf16),
            pltpu.VMEM((4, 6) + part, bf16),
            pltpu.VMEM((steps, 2) + part, bf16),
            pltpu.VMEM((steps, 4) + part, bf16),
            pltpu.VMEM((4, 2) + part, f32),
            pltpu.VMEM((2, 2) + part, f32),
            pltpu.VMEM((steps, 4) + part, bf16),
            pltpu.VMEM((4, 3, slots, wide), bf16),
            pltpu.VMEM((4, 3, slots, wide), bf16),
            pltpu.VMEM((4, 2, slots, half), bf16),
            pltpu.VMEM((8, slots, half), bf16),
            dma(()), dma((16,)), dma((16,)),
            dma((steps,)), dma((steps,)), dma((steps,)), dma((steps,)),
            dma((steps,)), dma((steps,)), dma((steps,)), dma((steps,)), dma((steps,)),
            dma((steps,)), dma((steps,)),
            dma((12,)), dma((12,)), dma((8,)), dma((8,)),
        ],
        compiler_params=pltpu.CompilerParams(
            has_side_effects=True, collective_id=0, vmem_limit_bytes=67043328
        ),
    )(tokens, routes, combine, gate, up, down)


def solution(mesh):
    placed = (
        P("fsdp", None),
        P("fsdp", None),
        P("fsdp", None),
        P("member", None, "fsdp"),
        P("member", None, "fsdp"),
        P("member", None, "fsdp"),
    )
    return jax.shard_map(
        body, mesh=mesh, in_specs=placed, out_specs=P("fsdp", "member"), check_vma=False
    )
```

```python
import jax
import jax.numpy as jnp
from jax import lax
from jax.experimental import pallas as pl
from jax.experimental.pallas import tpu as pltpu
from jax.sharding import PartitionSpec as P

PIECE = 256
AHEAD = 6
LAG = 7
MESH = pl.DeviceIdType.MESH


def contract(a, b, dims):
    return lax.dot_general(a, b, (dims, ((), ())), preferred_element_type=jnp.float32)


def kernel(
    tokens, routes, combine, gate, up, down, out,
    tokv, packed, tokbuf, tok, acc, wgu, wd, ps, rl, pr, own, keep, hb, osb, orv, fin, frv,
    t_c, tok_s, tok_r, gu_s, gu_r, d_s, d_r, p_s, l_r, p_r, h_s, h_r, q_s, q_r, o_s, o_r, f_s, f_r,
):
    steps = wgu.shape[0]
    slots = packed.shape[0]
    wide = tok.shape[1]
    group = tok.shape[0] // 4
    half = out.shape[1]
    count = tokv.shape[0]
    me = lax.axis_index("member")
    shard = lax.axis_index("fsdp")
    z, x = shard // 4, shard % 4

    share_rows = gate.shape[0] // 4
    short = share_rows - (steps - 1) * PIECE

    def span(xt, c):
        if isinstance(c, int) and c == 0:
            return pl.ds(pl.multiple_of(xt * share_rows, 64), short)
        return pl.ds(pl.multiple_of(xt * share_rows + short + (c - 1) * PIECE, 64), PIECE)

    def filled(ref, c):
        return ref.at[0:short] if isinstance(c, int) and c == 0 else ref

    def wait(ref, sem):
        pltpu.make_async_copy(ref, ref, sem).wait()

    def remote(src, dst, send, recv, zt, xt):
        pltpu.make_async_remote_copy(
            src, dst, send, recv, device_id={"fsdp": zt * 4 + xt}, device_id_type=MESH
        ).start()

    def columns(zt):
        return packed.at[:, pl.ds(pl.multiple_of(zt * wide, wide), wide)]

    def send_gate_up(c):
        for dx in (2, 1, 3):
            xt = (x + dx) % 4
            for w, ref in enumerate((gate, up)):
                remote(
                    ref.at[span(xt, c)], filled(wgu.at[c, x, w], c),
                    gu_s.at[c], gu_r.at[c], z, xt,
                )
        for w, ref in enumerate((gate, up)):
            pltpu.make_async_copy(
                ref.at[span(x, c)], filled(wgu.at[c, x, w], c), gu_r.at[c]
            ).start()

    def send_down(c):
        for dx in (2, 1, 3):
            xt = (x + dx) % 4
            remote(down.at[span(xt, c)], filled(wd.at[c, x], c), d_s.at[c], d_r.at[c], z, xt)
        pltpu.make_async_copy(down.at[span(x, c)], filled(wd.at[c, x], c), d_r.at[c]).start()

    barrier = pltpu.get_barrier_semaphore()
    for hop in range(1, 16):
        pl.semaphore_signal(
            barrier, inc=1, device_id={"fsdp": (shard + hop) % 16}, device_id_type=MESH
        )
    inside = me // 2 == z
    for m in range(8):
        @pl.when(jnp.logical_not(jnp.logical_and(inside, me == m)))
        def _():
            pl.semaphore_signal(
                barrier, inc=1, device_id={"member": m, "fsdp": (me // 2) * 4 + x},
                device_id_type=MESH,
            )

    load = pltpu.make_async_copy(tokens, tokv, t_c)
    load.start()
    wgu[0, :, :, short:, :] = jnp.zeros((4, 2, PIECE - short, PIECE), wgu.dtype)
    wd[0, :, short:, :] = jnp.zeros((4, PIECE - short, PIECE), wd.dtype)

    lanes = lax.broadcasted_iota(jnp.int32, (count, 128), 1)
    earlier = lax.broadcasted_iota(jnp.int32, (count, count), 0) >= (
        lax.broadcasted_iota(jnp.int32, (count, count), 1)
    )
    line = lax.broadcasted_iota(jnp.int32, (128, count), 0)
    table = jnp.where(line == 0, routes[0:1, :], routes[1:2, :]).astype(jnp.float32)
    table = jnp.where(line == 2, combine[0:1, :], table)
    table = jnp.where(line == 3, combine[1:2, :], table).T
    pair = [table[:, k : k + 1].astype(jnp.int32) for k in range(2)]
    share_of = [table[:, k : k + 1] for k in (2, 3)]
    named = jnp.logical_or(pair[0] == lanes, pair[1] == lanes)
    order = contract(
        earlier.astype(jnp.bfloat16), named.astype(jnp.bfloat16), ((1,), (0,))
    ).astype(jnp.int32)
    mine = jnp.sum(jnp.where(jnp.logical_and(named, lanes == me), order, 0), axis=1, keepdims=True)
    placed = jnp.where(mine - 1 == lanes, 1.0, 0.0).T[0:slots].astype(jnp.bfloat16)
    load.wait()
    for q in range(4):
        cols = slice(q * wide, (q + 1) * wide)
        packed[:, cols] = contract(placed, tokv[:, cols], ((1,), (0,))).astype(packed.dtype)

    @pl.when(inside)
    def _():
        pl.semaphore_wait(barrier, 22)

    @pl.when(jnp.logical_not(inside))
    def _():
        pl.semaphore_wait(barrier, 23)

    for dz in (2, 1, 3):
        zt = (z + dz) % 4
        remote(columns(zt), tokbuf.at[shard], tok_s.at[dz], tok_r.at[shard], zt, x)
    pltpu.make_async_copy(columns(z), tokbuf.at[shard], tok_r.at[shard]).start()
    send_gate_up(0)
    for dz in (2, 1, 3, 0):
        f = ((z + dz) % 4) * 4 + x
        wait(tokbuf.at[f], tok_r.at[f])
        for dx in (2, 1, 3):
            remote(
                tokbuf.at[f], tokbuf.at[f], tok_s.at[3 + dz * 3 + dx], tok_r.at[f],
                z, (x + dx) % 4,
            )
    for c in range(1, AHEAD + 1):
        send_gate_up(c)
    send_down(0)

    def unpack(dz):
        zt = (z + dz) % 4
        for dx in (0, 1, 3, 2):
            f = zt * 4 + (x + dx) % 4
            if dx:
                wait(tokbuf.at[f], tok_r.at[f])
            acc[pl.ds(pl.multiple_of(f * slots, 8), slots), :] = tokbuf[f].astype(jnp.float32)
        rows = pl.ds(pl.multiple_of(zt * group, 16), group)
        tok[rows, :] = acc[rows, :].astype(tok.dtype)

    def partial_sums(i):
        slot = i % 4
        first = isinstance(i, int)
        ready = (lambda dz: unpack(dz)) if first else (lambda dz: None)
        if first:
            ready(2)
            wait(wgu.at[0, :, :, 0:short], gu_r.at[0])
        else:
            wait(wgu.at[i], gu_r.at[i])

            @pl.when(i >= 4)
            def _():
                wait(ps.at[slot], p_s.at[i - 4])

        def share(dz, w):
            rows = pl.ds(pl.multiple_of(((z + dz) % 4) * group, 16), group)
            total = contract(tok[rows, 0:PIECE], wgu[i, 0, w], ((1,), (1,)))
            for k in range(1, 4):
                total += contract(
                    tok[rows, k * PIECE : (k + 1) * PIECE], wgu[i, k, w], ((1,), (1,))
                )
            return total

        def emit(n, dz, w, dst, sem, to):
            ps[slot, n] = share(dz, w).astype(ps.dtype)
            remote(ps.at[slot, n], dst, p_s.at[i], sem, (z + to) % 4, x)

        emit(0, 2, 0, rl.at[i, 0], l_r.at[i], 1)
        emit(1, 2, 1, rl.at[i, 1], l_r.at[i], 3)
        ready(1)
        emit(2, 1, 1, pr.at[i, 0], p_r.at[i], 1)
        ready(3)
        emit(3, 3, 0, pr.at[i, 1], p_r.at[i], 3)
        ready(0)
        keep[i % 2, 0] = share(1, 0)
        keep[i % 2, 1] = share(3, 1)
        own[i % 4, 0] = share(0, 0)
        own[i % 4, 1] = share(0, 1)

    def merge(j):
        wait(rl.at[j], l_r.at[j])
        for w, to in ((0, 1), (1, 3)):
            total = keep[j % 2, w] + rl[j, w].astype(jnp.float32)
            ps[j % 4, 4 + w] = total.astype(ps.dtype)
            remote(ps.at[j % 4, 4 + w], pr.at[j, 2 + w], p_s.at[j], p_r.at[j], (z + to) % 4, x)

    def activate(j):
        wait(pr.at[j], p_r.at[j])
        sums = [
            own[j % 4, w] + pr[j, 1 - w].astype(jnp.float32) + pr[j, 2 + w].astype(jnp.float32)
            for w in range(2)
        ]
        hidden = sums[0] / (1.0 + jnp.exp(-sums[0])) * sums[1]
        hb[j, z] = hidden.astype(hb.dtype)
        for dz in (1, 3):
            remote(hb.at[j, z], hb.at[j, z], h_s.at[j], h_r.at[j], (z + dz) % 4, x)

    def forward(j):
        wait(hb.at[j, 0:2], h_r.at[j])
        for dz, lo in ((1, 0), (3, group // 2)):
            piece = hb.at[j, (z - dz + 4) % 4, pl.ds(lo, group // 2)]
            remote(piece, piece, q_s.at[j], q_r.at[j], (z + dz) % 4, x)

    def project(k):
        wait(hb.at[k, 0], q_r.at[k])

        @pl.when(k == 0)
        def _():
            wait(wd.at[0, :, 0:short], d_r.at[0])

        @pl.when(k > 0)
        def _():
            wait(wd.at[k], d_r.at[k])

        for g in range(4):
            rows = pl.ds(g * group, group)
            for b in range(4):
                cols = slice(b * PIECE, (b + 1) * PIECE)
                acc[rows, cols] += contract(hb[k, g], wd[k, b], ((1,), (0,)))

    def step(i, carry):
        @pl.when(i + AHEAD < steps)
        def _():
            send_gate_up(i + AHEAD)

        @pl.when(i < steps)
        def _():
            send_down(i)
            partial_sums(i)

        @pl.when(i < steps + 1)
        def _():
            merge(i - 1)

        @pl.when(jnp.logical_and(i >= 2, i < steps + 2))
        def _():
            activate(i - 2)

        @pl.when(jnp.logical_and(i >= 3, i < steps + 3))
        def _():
            forward(i - 3)

        @pl.when(i >= LAG)
        def _():
            project(i - LAG)

        return carry

    partial_sums(0)
    acc[...] = jnp.zeros_like(acc)
    lax.fori_loop(1, steps + LAG, step, 0)

    for dzb in (2, 1, 3, 0):
        zb = (z + dzb) % 4
        for dx in (2, 1, 3):
            xt = (x + dx) % 4
            rows = pl.ds(pl.multiple_of((zb * 4 + xt) * slots, 8), slots)
            osb[dzb, dx - 1] = acc[rows, :].astype(osb.dtype)
            remote(
                osb.at[dzb, dx - 1], orv.at[dzb, dx - 1],
                o_s.at[dzb * 3 + dx - 1], o_r.at[dzb * 3 + dx - 1], z, xt,
            )
    for dzb in (2, 1, 3, 0):
        zb = (z + dzb) % 4
        rows = pl.ds(pl.multiple_of((zb * 4 + x) * slots, 8), slots)
        total = acc[rows, :]
        for s in range(3):
            wait(orv.at[dzb, s], o_r.at[dzb * 3 + s])
            total += orv[dzb, s].astype(jnp.float32)
        for h in range(2):
            n = dzb * 2 + h
            fin[dzb, h] = total[:, h * half : (h + 1) * half].astype(fin.dtype)

            def leave(n=n, h=h, dzb=dzb, zb=zb):
                pltpu.make_async_remote_copy(
                    fin.at[dzb, h], frv.at[me], f_s.at[n], f_r.at[me],
                    device_id={"member": 2 * z + h, "fsdp": zb * 4 + x}, device_id_type=MESH,
                ).start()

            if dzb:
                leave()
            else:
                pl.when(me != 2 * z + h)(leave)

                @pl.when(me == 2 * z + h)
                def _():
                    pltpu.make_async_copy(fin.at[dzb, h], frv.at[me], f_r.at[me]).start()

    mixed = jnp.zeros((count, half), jnp.float32)
    for m in range(8):
        pick = jnp.where(
            jnp.logical_and(order[:, m : m + 1] - 1 == lanes, named[:, m : m + 1]), 1.0, 0.0
        )[:, 0:slots].astype(jnp.bfloat16)
        scale = jnp.where(pair[0] == m, share_of[0], 0.0) + jnp.where(
            pair[1] == m, share_of[1], 0.0
        )
        wait(frv.at[m], f_r.at[m])
        mixed += scale * contract(pick, frv[m], ((1,), (0,)))
    out[...] = mixed.astype(out.dtype)

    for dzb in range(4):
        for h in range(2):
            if dzb:
                wait(fin.at[dzb, h], f_s.at[dzb * 2 + h])
            else:
                @pl.when(me != 2 * z + h)
                def _():
                    wait(fin.at[dzb, h], f_s.at[dzb * 2 + h])
        for s in range(3):
            wait(osb.at[dzb, s], o_s.at[dzb * 3 + s])
    for hop in range(1, 16):
        wait(tokbuf.at[0], tok_s.at[hop])
    wait(wgu.at[0, 0:3, :, 0:short], gu_s.at[0])
    wait(wd.at[0, 0:3, 0:short], d_s.at[0])

    def finish(c, carry):
        @pl.when(c >= 1)
        def _():
            wait(wgu.at[c, 0:3], gu_s.at[c])
            wait(wd.at[c, 0:3], d_s.at[c])

        wait(hb.at[c, 0:2], h_s.at[c])
        wait(hb.at[c, 0], q_s.at[c])

        @pl.when(c >= steps - 4)
        def _():
            wait(ps.at[c % 4], p_s.at[c])

        return carry

    lax.fori_loop(0, steps, finish, 0)


def body(tokens, routes, combine, gate_weight, up_weight, down_weight):
    count, features = tokens.shape
    experts = lax.axis_size("member")
    gate, up, down = gate_weight[0], up_weight[0], down_weight[0]
    slots, wide, half = 3 * count // experts, features // 4, features // 8
    rows = 16 * slots
    steps = -(-gate.shape[0] // (4 * PIECE))
    bf16, f32 = jnp.bfloat16, jnp.float32
    dma = pltpu.SemaphoreType.DMA
    whole = pl.BlockSpec(memory_space=pltpu.VMEM)
    away = pl.BlockSpec(memory_space=pl.ANY)
    part = (rows // 4, PIECE)
    return pl.pallas_call(
        kernel,
        out_shape=jax.ShapeDtypeStruct((count, half), bf16),
        in_specs=[away, whole, whole, away, away, away],
        out_specs=whole,
        scratch_shapes=[
            pltpu.VMEM((count, features), bf16),
            pltpu.VMEM((slots, features), bf16),
            pltpu.VMEM((16, slots, wide), bf16),
            pltpu.VMEM((rows, wide), bf16),
            pltpu.VMEM((rows, wide), f32),
            pltpu.VMEM((steps, 4, 2, PIECE, PIECE), bf16),
            pltpu.VMEM((steps, 4, PIECE, PIECE), bf16),
            pltpu.VMEM((4, 6) + part, bf16),
            pltpu.VMEM((steps, 2) + part, bf16),
            pltpu.VMEM((steps, 4) + part, bf16),
            pltpu.VMEM((4, 2) + part, f32),
            pltpu.VMEM((2, 2) + part, f32),
            pltpu.VMEM((steps, 4) + part, bf16),
            pltpu.VMEM((4, 3, slots, wide), bf16),
            pltpu.VMEM((4, 3, slots, wide), bf16),
            pltpu.VMEM((4, 2, slots, half), bf16),
            pltpu.VMEM((8, slots, half), bf16),
            dma(()), dma((16,)), dma((16,)),
            dma((steps,)), dma((steps,)), dma((steps,)), dma((steps,)),
            dma((steps,)), dma((steps,)), dma((steps,)), dma((steps,)), dma((steps,)),
            dma((steps,)), dma((steps,)),
            dma((12,)), dma((12,)), dma((8,)), dma((8,)),
        ],
        compiler_params=pltpu.CompilerParams(
            has_side_effects=True, collective_id=0, vmem_limit_bytes=67043328
        ),
    )(tokens, routes.T, combine.T, gate, up, down)


def solution(mesh):
    placed = (
        P("fsdp", None),
        P("fsdp", None),
        P("fsdp", None),
        P("member", None, "fsdp"),
        P("member", None, "fsdp"),
        P("member", None, "fsdp"),
    )
    return jax.shard_map(
        body, mesh=mesh, in_specs=placed, out_specs=P("fsdp", "member"), check_vma=False
    )
```

```python
import jax
import jax.numpy as jnp
from jax import lax
from jax.experimental import pallas as pl
from jax.experimental.pallas import tpu as pltpu
from jax.sharding import PartitionSpec as P

PIECE = 256
AHEAD = 6
LAG = 7
MESH = pl.DeviceIdType.MESH


def contract(a, b, dims):
    return lax.dot_general(a, b, (dims, ((), ())), preferred_element_type=jnp.float32)


def kernel(
    tokens, routes, combine, gate, up, down, out,
    tokv, packed, tokbuf, tok, acc, wgu, wd, ps, rl, pr, own, keep, hb, osb, orv, fin, frv,
    t_c, tok_s, tok_r, fw_s, fw_r, gu_s, gu_r, d_s, d_r, p_s, l_r, p_r, h_s, h_r, q_s, q_r, o_s, o_r, f_s, f_r,
):
    steps = wgu.shape[0]
    slots = packed.shape[0]
    wide = tok.shape[1]
    group = tok.shape[0] // 4
    half = out.shape[1]
    count = tokv.shape[0]
    me = lax.axis_index("member")
    shard = lax.axis_index("fsdp")
    z, x = shard // 4, shard % 4

    share_rows = gate.shape[0] // 4
    short = share_rows - (steps - 1) * PIECE

    def span(xt, c):
        if isinstance(c, int) and c == 0:
            return pl.ds(pl.multiple_of(xt * share_rows, 64), short)
        return pl.ds(pl.multiple_of(xt * share_rows + short + (c - 1) * PIECE, 64), PIECE)

    def filled(ref, c):
        return ref.at[0:short] if isinstance(c, int) and c == 0 else ref

    def wait(ref, sem):
        pltpu.make_async_copy(ref, ref, sem).wait()

    def remote(src, dst, send, recv, zt, xt):
        pltpu.make_async_remote_copy(
            src, dst, send, recv, device_id={"fsdp": zt * 4 + xt}, device_id_type=MESH
        ).start()

    def columns(zt):
        return packed.at[:, pl.ds(pl.multiple_of(zt * wide, wide), wide)]

    def send_gate_up(c):
        for dx in (2, 1, 3):
            xt = (x + dx) % 4
            for w, ref in enumerate((gate, up)):
                remote(
                    ref.at[span(xt, c)], filled(wgu.at[c, x, w], c),
                    gu_s.at[c], gu_r.at[c], z, xt,
                )
        for w, ref in enumerate((gate, up)):
            pltpu.make_async_copy(
                ref.at[span(x, c)], filled(wgu.at[c, x, w], c), gu_r.at[c]
            ).start()

    def send_down(c):
        for dx in (2, 1, 3):
            xt = (x + dx) % 4
            remote(down.at[span(xt, c)], filled(wd.at[c, x], c), d_s.at[c], d_r.at[c], z, xt)
        pltpu.make_async_copy(down.at[span(x, c)], filled(wd.at[c, x], c), d_r.at[c]).start()

    barrier = pltpu.get_barrier_semaphore()
    for hop in range(1, 16):
        pl.semaphore_signal(
            barrier, inc=1, device_id={"fsdp": (shard + hop) % 16}, device_id_type=MESH
        )
    inside = me // 2 == z
    for m in range(8):
        @pl.when(jnp.logical_not(jnp.logical_and(inside, me == m)))
        def _():
            pl.semaphore_signal(
                barrier, inc=1, device_id={"member": m, "fsdp": (me // 2) * 4 + x},
                device_id_type=MESH,
            )

    load = pltpu.make_async_copy(tokens, tokv, t_c)
    load.start()
    wgu[0, :, :, short:, :] = jnp.zeros((4, 2, PIECE - short, PIECE), wgu.dtype)
    wd[0, :, short:, :] = jnp.zeros((4, PIECE - short, PIECE), wd.dtype)

    lanes = lax.broadcasted_iota(jnp.int32, (count, 128), 1)
    earlier = lax.broadcasted_iota(jnp.int32, (count, count), 0) >= (
        lax.broadcasted_iota(jnp.int32, (count, count), 1)
    )
    line = lax.broadcasted_iota(jnp.int32, (128, count), 0)
    table = jnp.where(line == 0, routes[0:1, :], routes[1:2, :]).astype(jnp.float32)
    table = jnp.where(line == 2, combine[0:1, :], table)
    table = jnp.where(line == 3, combine[1:2, :], table).T
    pair = [table[:, k : k + 1].astype(jnp.int32) for k in range(2)]
    share_of = [table[:, k : k + 1] for k in (2, 3)]
    named = jnp.logical_or(pair[0] == lanes, pair[1] == lanes)
    order = contract(
        earlier.astype(jnp.bfloat16), named.astype(jnp.bfloat16), ((1,), (0,))
    ).astype(jnp.int32)
    mine = jnp.sum(jnp.where(jnp.logical_and(named, lanes == me), order, 0), axis=1, keepdims=True)
    placed = jnp.where(mine - 1 == lanes, 1.0, 0.0).T[0:slots].astype(jnp.bfloat16)
    load.wait()
    for q in range(4):
        cols = slice(q * wide, (q + 1) * wide)
        packed[:, cols] = contract(placed, tokv[:, cols], ((1,), (0,))).astype(packed.dtype)

    @pl.when(inside)
    def _():
        pl.semaphore_wait(barrier, 22)

    @pl.when(jnp.logical_not(inside))
    def _():
        pl.semaphore_wait(barrier, 23)

    for dz in (2, 1, 3):
        zt = (z + dz) % 4
        remote(columns(zt), tokbuf.at[shard], tok_s.at[dz], tok_r.at[shard], zt, x)
    pltpu.make_async_copy(columns(z), tokbuf.at[shard], tok_r.at[shard]).start()
    send_gate_up(0)
    for dz in (2, 1, 3, 0):
        f = ((z + dz) % 4) * 4 + x
        wait(tokbuf.at[f], tok_r.at[f])
        for dx in (2, 1, 3) if dz == 2 else (1, 3):
            remote(
                tokbuf.at[f], tokbuf.at[f], tok_s.at[3 + dz * 3 + dx], tok_r.at[f],
                z, (x + dx) % 4,
            )
    send_gate_up(1)

    def hand_on(dz):
        for n, dx in enumerate((1, 3)):
            f = ((z + dz) % 4) * 4 + (x - dx + 4) % 4
            wait(tokbuf.at[f], tok_r.at[f])
            piece = tokbuf.at[f, :, n * (wide // 2) : (n + 1) * (wide // 2)]
            remote(piece, piece, fw_s.at[dz * 2 + n], fw_r.at[dz * 2 + n], z, (x + dx) % 4)

    def unpack(dz):
        zt = (z + dz) % 4
        for dx in (0, 1, 3, 2):
            f = zt * 4 + (x + dx) % 4
            if dz != 2 and dx == 2:
                for n in range(2):
                    wait(tokbuf.at[f, :, 0 : wide // 2], fw_r.at[dz * 2 + n])
            elif dz == 2 and dx:
                wait(tokbuf.at[f], tok_r.at[f])
            acc[pl.ds(pl.multiple_of(f * slots, 8), slots), :] = tokbuf[f].astype(jnp.float32)
        rows = pl.ds(pl.multiple_of(zt * group, 16), group)
        tok[rows, :] = acc[rows, :].astype(tok.dtype)

    def partial_sums(i):
        slot = i % 4
        first = isinstance(i, int)
        ready = (lambda dz: unpack(dz)) if first else (lambda dz: None)
        if first:
            ready(2)
            wait(wgu.at[0, :, :, 0:short], gu_r.at[0])
        else:
            wait(wgu.at[i], gu_r.at[i])

            @pl.when(i >= 4)
            def _():
                wait(ps.at[slot], p_s.at[i - 4])

        def share(dz, w):
            rows = pl.ds(pl.multiple_of(((z + dz) % 4) * group, 16), group)
            total = contract(tok[rows, 0:PIECE], wgu[i, 0, w], ((1,), (1,)))
            for k in range(1, 4):
                total += contract(
                    tok[rows, k * PIECE : (k + 1) * PIECE], wgu[i, k, w], ((1,), (1,))
                )
            return total

        def emit(n, dz, w, dst, sem, to):
            ps[slot, n] = share(dz, w).astype(ps.dtype)
            remote(ps.at[slot, n], dst, p_s.at[i], sem, (z + to) % 4, x)

        emit(0, 2, 0, rl.at[i, 0], l_r.at[i], 1)
        emit(1, 2, 1, rl.at[i, 1], l_r.at[i], 3)
        if first:
            for dz in (1, 3, 0):
                hand_on(dz)
            for c in range(2, AHEAD + 1):
                send_gate_up(c)
            send_down(0)
        ready(1)
        emit(2, 1, 1, pr.at[i, 0], p_r.at[i], 1)
        ready(3)
        emit(3, 3, 0, pr.at[i, 1], p_r.at[i], 3)
        ready(0)
        keep[i % 2, 0] = share(1, 0)
        keep[i % 2, 1] = share(3, 1)
        own[i % 4, 0] = share(0, 0)
        own[i % 4, 1] = share(0, 1)

    def merge(j):
        wait(rl.at[j], l_r.at[j])
        for w, to in ((0, 1), (1, 3)):
            total = keep[j % 2, w] + rl[j, w].astype(jnp.float32)
            ps[j % 4, 4 + w] = total.astype(ps.dtype)
            remote(ps.at[j % 4, 4 + w], pr.at[j, 2 + w], p_s.at[j], p_r.at[j], (z + to) % 4, x)

    def activate(j):
        wait(pr.at[j], p_r.at[j])
        sums = [
            own[j % 4, w] + pr[j, 1 - w].astype(jnp.float32) + pr[j, 2 + w].astype(jnp.float32)
            for w in range(2)
        ]
        hidden = sums[0] / (1.0 + jnp.exp(-sums[0])) * sums[1]
        hb[j, z] = hidden.astype(hb.dtype)
        for dz in (1, 3):
            remote(hb.at[j, z], hb.at[j, z], h_s.at[j], h_r.at[j], (z + dz) % 4, x)

    def forward(j):
        wait(hb.at[j, 0:2], h_r.at[j])
        for dz, lo in ((1, 0), (3, group // 2)):
            piece = hb.at[j, (z - dz + 4) % 4, pl.ds(lo, group // 2)]
            remote(piece, piece, q_s.at[j], q_r.at[j], (z + dz) % 4, x)

    def project(k):
        wait(hb.at[k, 0], q_r.at[k])

        @pl.when(k == 0)
        def _():
            wait(wd.at[0, :, 0:short], d_r.at[0])

        @pl.when(k > 0)
        def _():
            wait(wd.at[k], d_r.at[k])

        for g in range(4):
            rows = pl.ds(g * group, group)
            for b in range(4):
                cols = slice(b * PIECE, (b + 1) * PIECE)
                acc[rows, cols] += contract(hb[k, g], wd[k, b], ((1,), (0,)))

    def step(i, carry):
        @pl.when(i + AHEAD < steps)
        def _():
            send_gate_up(i + AHEAD)

        @pl.when(i < steps)
        def _():
            send_down(i)
            partial_sums(i)

        @pl.when(i < steps + 1)
        def _():
            merge(i - 1)

        @pl.when(jnp.logical_and(i >= 2, i < steps + 2))
        def _():
            activate(i - 2)

        @pl.when(jnp.logical_and(i >= 3, i < steps + 3))
        def _():
            forward(i - 3)

        @pl.when(i >= LAG)
        def _():
            project(i - LAG)

        return carry

    partial_sums(0)
    acc[...] = jnp.zeros_like(acc)
    lax.fori_loop(1, steps + LAG, step, 0)

    for dzb in (2, 1, 3, 0):
        zb = (z + dzb) % 4
        for dx in (2, 1, 3):
            xt = (x + dx) % 4
            rows = pl.ds(pl.multiple_of((zb * 4 + xt) * slots, 8), slots)
            osb[dzb, dx - 1] = acc[rows, :].astype(osb.dtype)
            remote(
                osb.at[dzb, dx - 1], orv.at[dzb, dx - 1],
                o_s.at[dzb * 3 + dx - 1], o_r.at[dzb * 3 + dx - 1], z, xt,
            )
    for dzb in (2, 1, 3, 0):
        zb = (z + dzb) % 4
        rows = pl.ds(pl.multiple_of((zb * 4 + x) * slots, 8), slots)
        total = acc[rows, :]
        for s in range(3):
            wait(orv.at[dzb, s], o_r.at[dzb * 3 + s])
            total += orv[dzb, s].astype(jnp.float32)
        for h in range(2):
            n = dzb * 2 + h
            fin[dzb, h] = total[:, h * half : (h + 1) * half].astype(fin.dtype)

            def leave(n=n, h=h, dzb=dzb, zb=zb):
                pltpu.make_async_remote_copy(
                    fin.at[dzb, h], frv.at[me], f_s.at[n], f_r.at[me],
                    device_id={"member": 2 * z + h, "fsdp": zb * 4 + x}, device_id_type=MESH,
                ).start()

            if dzb:
                leave()
            else:
                pl.when(me != 2 * z + h)(leave)

                @pl.when(me == 2 * z + h)
                def _():
                    pltpu.make_async_copy(fin.at[dzb, h], frv.at[me], f_r.at[me]).start()

    mixed = jnp.zeros((count, half), jnp.float32)
    for m in range(8):
        pick = jnp.where(
            jnp.logical_and(order[:, m : m + 1] - 1 == lanes, named[:, m : m + 1]), 1.0, 0.0
        )[:, 0:slots].astype(jnp.bfloat16)
        scale = jnp.where(pair[0] == m, share_of[0], 0.0) + jnp.where(
            pair[1] == m, share_of[1], 0.0
        )
        wait(frv.at[m], f_r.at[m])
        mixed += scale * contract(pick, frv[m], ((1,), (0,)))
    out[...] = mixed.astype(out.dtype)

    for dzb in range(4):
        for h in range(2):
            if dzb:
                wait(fin.at[dzb, h], f_s.at[dzb * 2 + h])
            else:
                @pl.when(me != 2 * z + h)
                def _():
                    wait(fin.at[dzb, h], f_s.at[dzb * 2 + h])
        for s in range(3):
            wait(osb.at[dzb, s], o_s.at[dzb * 3 + s])
    for hop in (1, 2, 3) + tuple(3 + dz * 3 + dx for dz in range(4) for dx in (1, 3)) + (11,):
        wait(tokbuf.at[0], tok_s.at[hop])
    for dz in (1, 3, 0):
        for n in range(2):
            wait(tokbuf.at[0, :, 0 : wide // 2], fw_s.at[dz * 2 + n])
    wait(wgu.at[0, 0:3, :, 0:short], gu_s.at[0])
    wait(wd.at[0, 0:3, 0:short], d_s.at[0])

    def finish(c, carry):
        @pl.when(c >= 1)
        def _():
            wait(wgu.at[c, 0:3], gu_s.at[c])
            wait(wd.at[c, 0:3], d_s.at[c])

        wait(hb.at[c, 0:2], h_s.at[c])
        wait(hb.at[c, 0], q_s.at[c])

        @pl.when(c >= steps - 4)
        def _():
            wait(ps.at[c % 4], p_s.at[c])

        return carry

    lax.fori_loop(0, steps, finish, 0)


def body(tokens, routes, combine, gate_weight, up_weight, down_weight):
    count, features = tokens.shape
    experts = lax.axis_size("member")
    gate, up, down = gate_weight[0], up_weight[0], down_weight[0]
    slots, wide, half = 3 * count // experts, features // 4, features // 8
    rows = 16 * slots
    steps = -(-gate.shape[0] // (4 * PIECE))
    bf16, f32 = jnp.bfloat16, jnp.float32
    dma = pltpu.SemaphoreType.DMA
    whole = pl.BlockSpec(memory_space=pltpu.VMEM)
    away = pl.BlockSpec(memory_space=pl.ANY)
    part = (rows // 4, PIECE)
    return pl.pallas_call(
        kernel,
        out_shape=jax.ShapeDtypeStruct((count, half), bf16),
        in_specs=[away, whole, whole, away, away, away],
        out_specs=whole,
        scratch_shapes=[
            pltpu.VMEM((count, features), bf16),
            pltpu.VMEM((slots, features), bf16),
            pltpu.VMEM((16, slots, wide), bf16),
            pltpu.VMEM((rows, wide), bf16),
            pltpu.VMEM((rows, wide), f32),
            pltpu.VMEM((steps, 4, 2, PIECE, PIECE), bf16),
            pltpu.VMEM((steps, 4, PIECE, PIECE), bf16),
            pltpu.VMEM((4, 6) + part, bf16),
            pltpu.VMEM((steps, 2) + part, bf16),
            pltpu.VMEM((steps, 4) + part, bf16),
            pltpu.VMEM((4, 2) + part, f32),
            pltpu.VMEM((2, 2) + part, f32),
            pltpu.VMEM((steps, 4) + part, bf16),
            pltpu.VMEM((4, 3, slots, wide), bf16),
            pltpu.VMEM((4, 3, slots, wide), bf16),
            pltpu.VMEM((4, 2, slots, half), bf16),
            pltpu.VMEM((8, slots, half), bf16),
            dma(()), dma((16,)), dma((16,)), dma((8,)), dma((8,)),
            dma((steps,)), dma((steps,)), dma((steps,)), dma((steps,)),
            dma((steps,)), dma((steps,)), dma((steps,)), dma((steps,)), dma((steps,)),
            dma((steps,)), dma((steps,)),
            dma((12,)), dma((12,)), dma((8,)), dma((8,)),
        ],
        compiler_params=pltpu.CompilerParams(
            has_side_effects=True, collective_id=0, vmem_limit_bytes=67043328
        ),
    )(tokens, routes.T, combine.T, gate, up, down)


def solution(mesh):
    placed = (
        P("fsdp", None),
        P("fsdp", None),
        P("fsdp", None),
        P("member", None, "fsdp"),
        P("member", None, "fsdp"),
        P("member", None, "fsdp"),
    )
    return jax.shard_map(
        body, mesh=mesh, in_specs=placed, out_specs=P("fsdp", "member"), check_vma=False
    )
```

```python
import jax
import jax.numpy as jnp
from jax import lax
from jax.experimental import pallas as pl
from jax.experimental.pallas import tpu as pltpu
from jax.sharding import PartitionSpec as P

PIECE = 256
AHEAD = 6
LAG = 7
MESH = pl.DeviceIdType.MESH


def contract(a, b, dims):
    return lax.dot_general(a, b, (dims, ((), ())), preferred_element_type=jnp.float32)


def kernel(
    tokens, routes, combine, gate, up, down, out,
    tokv, packed, tokbuf, tok, acc, wgu, wd, ps, rl, pr, own, keep, hb, osb, orv, fin, frv,
    t_c, tok_s, tok_r, fw_s, fw_r, gu_s, gu_r, d_s, d_r, p_s, l_r, p_r, h_s, h_r, q_s, q_r, o_s, o_r, f_s, f_r,
):
    steps = wgu.shape[0]
    slots = packed.shape[0]
    wide = tok.shape[1]
    group = tok.shape[0] // 4
    half = out.shape[1]
    count = tokv.shape[0]
    me = lax.axis_index("member")
    shard = lax.axis_index("fsdp")
    z, x = shard // 4, shard % 4

    share_rows = gate.shape[0] // 4
    short = share_rows - (steps - 1) * PIECE

    def span(xt, c):
        if isinstance(c, int) and c == 0:
            return pl.ds(pl.multiple_of(xt * share_rows, 64), short)
        return pl.ds(pl.multiple_of(xt * share_rows + short + (c - 1) * PIECE, 64), PIECE)

    def filled(ref, c):
        return ref.at[0:short] if isinstance(c, int) and c == 0 else ref

    def wait(ref, sem):
        pltpu.make_async_copy(ref, ref, sem).wait()

    def remote(src, dst, send, recv, zt, xt):
        pltpu.make_async_remote_copy(
            src, dst, send, recv, device_id={"fsdp": zt * 4 + xt}, device_id_type=MESH
        ).start()

    def columns(zt):
        return packed.at[:, pl.ds(pl.multiple_of(zt * wide, wide), wide)]

    def send_gate_up(c):
        for dx in (2, 1, 3):
            xt = (x + dx) % 4
            for w, ref in enumerate((gate, up)):
                remote(
                    ref.at[span(xt, c)], filled(wgu.at[c, x, w], c),
                    gu_s.at[c], gu_r.at[c], z, xt,
                )
        for w, ref in enumerate((gate, up)):
            pltpu.make_async_copy(
                ref.at[span(x, c)], filled(wgu.at[c, x, w], c), gu_r.at[c]
            ).start()

    def send_down(c):
        for dx in (2, 1, 3):
            xt = (x + dx) % 4
            remote(down.at[span(xt, c)], filled(wd.at[c, x], c), d_s.at[c], d_r.at[c], z, xt)
        pltpu.make_async_copy(down.at[span(x, c)], filled(wd.at[c, x], c), d_r.at[c]).start()

    barrier = pltpu.get_barrier_semaphore()
    for hop in range(1, 16):
        pl.semaphore_signal(
            barrier, inc=1, device_id={"fsdp": (shard + hop) % 16}, device_id_type=MESH
        )
    inside = me // 2 == z
    for m in range(8):
        @pl.when(jnp.logical_not(jnp.logical_and(inside, me == m)))
        def _():
            pl.semaphore_signal(
                barrier, inc=1, device_id={"member": m, "fsdp": (me // 2) * 4 + x},
                device_id_type=MESH,
            )

    load = pltpu.make_async_copy(tokens, tokv, t_c)
    load.start()
    wgu[0, :, :, short:, :] = jnp.zeros((4, 2, PIECE - short, PIECE), wgu.dtype)
    wd[0, :, short:, :] = jnp.zeros((4, PIECE - short, PIECE), wd.dtype)

    lanes = lax.broadcasted_iota(jnp.int32, (count, 128), 1)
    earlier = lax.broadcasted_iota(jnp.int32, (count, count), 0) >= (
        lax.broadcasted_iota(jnp.int32, (count, count), 1)
    )
    line = lax.broadcasted_iota(jnp.int32, (128, count), 0)
    table = jnp.where(line == 0, routes[0:1, :], routes[1:2, :]).astype(jnp.float32)
    table = jnp.where(line == 2, combine[0:1, :], table)
    table = jnp.where(line == 3, combine[1:2, :], table).T
    pair = [table[:, k : k + 1].astype(jnp.int32) for k in range(2)]
    share_of = [table[:, k : k + 1] for k in (2, 3)]
    named = jnp.logical_or(pair[0] == lanes, pair[1] == lanes)
    order = contract(
        earlier.astype(jnp.bfloat16), named.astype(jnp.bfloat16), ((1,), (0,))
    ).astype(jnp.int32)
    mine = jnp.sum(jnp.where(jnp.logical_and(named, lanes == me), order, 0), axis=1, keepdims=True)
    placed = jnp.where(mine - 1 == lanes, 1.0, 0.0).T[0:slots].astype(jnp.bfloat16)
    load.wait()
    for q in range(4):
        cols = slice(q * wide, (q + 1) * wide)
        packed[:, cols] = contract(placed, tokv[:, cols], ((1,), (0,))).astype(packed.dtype)

    @pl.when(inside)
    def _():
        pl.semaphore_wait(barrier, 22)

    @pl.when(jnp.logical_not(inside))
    def _():
        pl.semaphore_wait(barrier, 23)

    for dz in (2, 1, 3):
        zt = (z + dz) % 4
        remote(columns(zt), tokbuf.at[shard], tok_s.at[dz], tok_r.at[shard], zt, x)
    pltpu.make_async_copy(columns(z), tokbuf.at[shard], tok_r.at[shard]).start()
    send_gate_up(0)
    for dz in (2, 1, 3, 0):
        f = ((z + dz) % 4) * 4 + x
        wait(tokbuf.at[f], tok_r.at[f])
        for dx in (2, 1, 3) if dz == 2 else (1, 3):
            remote(
                tokbuf.at[f], tokbuf.at[f], tok_s.at[3 + dz * 3 + dx], tok_r.at[f],
                z, (x + dx) % 4,
            )
    send_gate_up(1)

    def hand_on(dz):
        for n, dx in enumerate((1, 3)):
            f = ((z + dz) % 4) * 4 + (x - dx + 4) % 4
            wait(tokbuf.at[f], tok_r.at[f])
            piece = tokbuf.at[f, :, n * (wide // 2) : (n + 1) * (wide // 2)]
            remote(piece, piece, fw_s.at[dz * 2 + n], fw_r.at[dz * 2 + n], z, (x + dx) % 4)

    def unpack(dz):
        zt = (z + dz) % 4
        for dx in (0, 1, 3, 2):
            f = zt * 4 + (x + dx) % 4
            if dz != 2 and dx == 2:
                for n in range(2):
                    wait(tokbuf.at[f, :, 0 : wide // 2], fw_r.at[dz * 2 + n])
            elif dz == 2 and dx:
                wait(tokbuf.at[f], tok_r.at[f])
            acc[pl.ds(pl.multiple_of(f * slots, 8), slots), :] = tokbuf[f].astype(jnp.float32)
        rows = pl.ds(pl.multiple_of(zt * group, 16), group)
        tok[rows, :] = acc[rows, :].astype(tok.dtype)

    def partial_sums(i):
        slot = i % 4
        first = isinstance(i, int)
        ready = (lambda dz: unpack(dz)) if first else (lambda dz: None)
        if first:
            ready(2)
            wait(wgu.at[0, :, :, 0:short], gu_r.at[0])
        else:
            wait(wgu.at[i], gu_r.at[i])

            @pl.when(i >= 4)
            def _():
                wait(ps.at[slot], p_s.at[i - 4])

        def share(dz, w):
            rows = pl.ds(pl.multiple_of(((z + dz) % 4) * group, 16), group)
            total = contract(tok[rows, 0:PIECE], wgu[i, 0, w], ((1,), (1,)))
            for k in range(1, 4):
                total += contract(
                    tok[rows, k * PIECE : (k + 1) * PIECE], wgu[i, k, w], ((1,), (1,))
                )
            return total

        def emit(n, dz, w, dst, sem, to):
            ps[slot, n] = share(dz, w).astype(ps.dtype)
            remote(ps.at[slot, n], dst, p_s.at[i], sem, (z + to) % 4, x)

        emit(0, 2, 0, rl.at[i, 0], l_r.at[i], 1)
        emit(1, 2, 1, rl.at[i, 1], l_r.at[i], 3)
        if first:
            for dz in (1, 3, 0):
                hand_on(dz)
            for c in range(2, AHEAD + 1):
                send_gate_up(c)
            send_down(0)
        ready(1)
        emit(2, 1, 1, pr.at[i, 0], p_r.at[i], 1)
        ready(3)
        emit(3, 3, 0, pr.at[i, 1], p_r.at[i], 3)
        ready(0)
        keep[i % 2, 0] = share(1, 0)
        keep[i % 2, 1] = share(3, 1)
        own[i % 4, 0] = share(0, 0)
        own[i % 4, 1] = share(0, 1)

    def merge(j):
        wait(rl.at[j], l_r.at[j])
        for w, to in ((0, 1), (1, 3)):
            total = keep[j % 2, w] + rl[j, w].astype(jnp.float32)
            ps[j % 4, 4 + w] = total.astype(ps.dtype)
            remote(ps.at[j % 4, 4 + w], pr.at[j, 2 + w], p_s.at[j], p_r.at[j], (z + to) % 4, x)

    def activate(j):
        wait(pr.at[j], p_r.at[j])
        sums = [
            own[j % 4, w] + pr[j, 1 - w].astype(jnp.float32) + pr[j, 2 + w].astype(jnp.float32)
            for w in range(2)
        ]
        hidden = sums[0] / (1.0 + jnp.exp(-sums[0])) * sums[1]
        hb[j, z] = hidden.astype(hb.dtype)
        for dz in (1, 3):
            remote(hb.at[j, z], hb.at[j, z], h_s.at[j], h_r.at[j], (z + dz) % 4, x)

    def forward(j):
        wait(hb.at[j, 0:2], h_r.at[j])
        for dz, lo in ((1, 0), (3, group // 2)):
            piece = hb.at[j, (z - dz + 4) % 4, pl.ds(lo, group // 2)]
            remote(piece, piece, q_s.at[j], q_r.at[j], (z + dz) % 4, x)

    def project(k):
        wait(hb.at[k, 0], q_r.at[k])

        @pl.when(k == 0)
        def _():
            wait(wd.at[0, :, 0:short], d_r.at[0])

        @pl.when(k > 0)
        def _():
            wait(wd.at[k], d_r.at[k])

        for g in range(4):
            rows = pl.ds(g * group, group)
            for b in range(4):
                cols = slice(b * PIECE, (b + 1) * PIECE)
                acc[rows, cols] += contract(hb[k, g], wd[k, b], ((1,), (0,)))

    def step(i, carry):
        @pl.when(i + AHEAD < steps)
        def _():
            send_gate_up(i + AHEAD)

        @pl.when(i < steps)
        def _():
            send_down(i)
            partial_sums(i)

        @pl.when(i < steps + 1)
        def _():
            merge(i - 1)

        @pl.when(jnp.logical_and(i >= 2, i < steps + 2))
        def _():
            activate(i - 2)

        @pl.when(jnp.logical_and(i >= 3, i < steps + 3))
        def _():
            forward(i - 3)

        late = i // steps
        k = i - LAG + late * (i - steps)

        @pl.when(i >= LAG)
        def _():
            project(k)

        @pl.when(jnp.logical_and(i >= steps, k + 1 < steps))
        def _():
            project(k + 1)

        return carry

    partial_sums(0)
    acc[...] = jnp.zeros_like(acc)
    lax.fori_loop(1, steps + (LAG + 1) // 2, step, 0)

    for dzb in (2, 1, 3, 0):
        zb = (z + dzb) % 4
        for dx in (2, 1, 3):
            xt = (x + dx) % 4
            rows = pl.ds(pl.multiple_of((zb * 4 + xt) * slots, 8), slots)
            osb[dzb, dx - 1] = acc[rows, :].astype(osb.dtype)
            remote(
                osb.at[dzb, dx - 1], orv.at[dzb, dx - 1],
                o_s.at[dzb * 3 + dx - 1], o_r.at[dzb * 3 + dx - 1], z, xt,
            )
    for dzb in (2, 1, 3, 0):
        zb = (z + dzb) % 4
        rows = pl.ds(pl.multiple_of((zb * 4 + x) * slots, 8), slots)
        total = acc[rows, :]
        for s in range(3):
            wait(orv.at[dzb, s], o_r.at[dzb * 3 + s])
            total += orv[dzb, s].astype(jnp.float32)
        for h in range(2):
            n = dzb * 2 + h
            fin[dzb, h] = total[:, h * half : (h + 1) * half].astype(fin.dtype)

            def leave(n=n, h=h, dzb=dzb, zb=zb):
                pltpu.make_async_remote_copy(
                    fin.at[dzb, h], frv.at[me], f_s.at[n], f_r.at[me],
                    device_id={"member": 2 * z + h, "fsdp": zb * 4 + x}, device_id_type=MESH,
                ).start()

            if dzb:
                leave()
            else:
                pl.when(me != 2 * z + h)(leave)

                @pl.when(me == 2 * z + h)
                def _():
                    pltpu.make_async_copy(fin.at[dzb, h], frv.at[me], f_r.at[me]).start()

    mixed = jnp.zeros((count, half), jnp.float32)
    for m in range(8):
        pick = jnp.where(
            jnp.logical_and(order[:, m : m + 1] - 1 == lanes, named[:, m : m + 1]), 1.0, 0.0
        )[:, 0:slots].astype(jnp.bfloat16)
        scale = jnp.where(pair[0] == m, share_of[0], 0.0) + jnp.where(
            pair[1] == m, share_of[1], 0.0
        )
        wait(frv.at[m], f_r.at[m])
        mixed += scale * contract(pick, frv[m], ((1,), (0,)))
    out[...] = mixed.astype(out.dtype)

    for dzb in range(4):
        for h in range(2):
            if dzb:
                wait(fin.at[dzb, h], f_s.at[dzb * 2 + h])
            else:
                @pl.when(me != 2 * z + h)
                def _():
                    wait(fin.at[dzb, h], f_s.at[dzb * 2 + h])
        for s in range(3):
            wait(osb.at[dzb, s], o_s.at[dzb * 3 + s])
    for hop in (1, 2, 3) + tuple(3 + dz * 3 + dx for dz in range(4) for dx in (1, 3)) + (11,):
        wait(tokbuf.at[0], tok_s.at[hop])
    for dz in (1, 3, 0):
        for n in range(2):
            wait(tokbuf.at[0, :, 0 : wide // 2], fw_s.at[dz * 2 + n])
    wait(wgu.at[0, 0:3, :, 0:short], gu_s.at[0])
    wait(wd.at[0, 0:3, 0:short], d_s.at[0])

    def finish(c, carry):
        @pl.when(c >= 1)
        def _():
            wait(wgu.at[c, 0:3], gu_s.at[c])
            wait(wd.at[c, 0:3], d_s.at[c])

        wait(hb.at[c, 0:2], h_s.at[c])
        wait(hb.at[c, 0], q_s.at[c])

        @pl.when(c >= steps - 4)
        def _():
            wait(ps.at[c % 4], p_s.at[c])

        return carry

    lax.fori_loop(0, steps, finish, 0)


def body(tokens, routes, combine, gate_weight, up_weight, down_weight):
    count, features = tokens.shape
    experts = lax.axis_size("member")
    gate, up, down = gate_weight[0], up_weight[0], down_weight[0]
    slots, wide, half = 3 * count // experts, features // 4, features // 8
    rows = 16 * slots
    steps = -(-gate.shape[0] // (4 * PIECE))
    bf16, f32 = jnp.bfloat16, jnp.float32
    dma = pltpu.SemaphoreType.DMA
    whole = pl.BlockSpec(memory_space=pltpu.VMEM)
    away = pl.BlockSpec(memory_space=pl.ANY)
    part = (rows // 4, PIECE)
    return pl.pallas_call(
        kernel,
        out_shape=jax.ShapeDtypeStruct((count, half), bf16),
        in_specs=[away, whole, whole, away, away, away],
        out_specs=whole,
        scratch_shapes=[
            pltpu.VMEM((count, features), bf16),
            pltpu.VMEM((slots, features), bf16),
            pltpu.VMEM((16, slots, wide), bf16),
            pltpu.VMEM((rows, wide), bf16),
            pltpu.VMEM((rows, wide), f32),
            pltpu.VMEM((steps, 4, 2, PIECE, PIECE), bf16),
            pltpu.VMEM((steps, 4, PIECE, PIECE), bf16),
            pltpu.VMEM((4, 6) + part, bf16),
            pltpu.VMEM((steps, 2) + part, bf16),
            pltpu.VMEM((steps, 4) + part, bf16),
            pltpu.VMEM((4, 2) + part, f32),
            pltpu.VMEM((2, 2) + part, f32),
            pltpu.VMEM((steps, 4) + part, bf16),
            pltpu.VMEM((4, 3, slots, wide), bf16),
            pltpu.VMEM((4, 3, slots, wide), bf16),
            pltpu.VMEM((4, 2, slots, half), bf16),
            pltpu.VMEM((8, slots, half), bf16),
            dma(()), dma((16,)), dma((16,)), dma((8,)), dma((8,)),
            dma((steps,)), dma((steps,)), dma((steps,)), dma((steps,)),
            dma((steps,)), dma((steps,)), dma((steps,)), dma((steps,)), dma((steps,)),
            dma((steps,)), dma((steps,)),
            dma((12,)), dma((12,)), dma((8,)), dma((8,)),
        ],
        compiler_params=pltpu.CompilerParams(
            has_side_effects=True, collective_id=0, vmem_limit_bytes=67043328
        ),
    )(tokens, routes.T, combine.T, gate, up, down)


def solution(mesh):
    placed = (
        P("fsdp", None),
        P("fsdp", None),
        P("fsdp", None),
        P("member", None, "fsdp"),
        P("member", None, "fsdp"),
        P("member", None, "fsdp"),
    )
    return jax.shard_map(
        body, mesh=mesh, in_specs=placed, out_specs=P("fsdp", "member"), check_vma=False
    )
```
